256 devices in a mesh: table: 16 (over z, core), seq: 16 (over x, y).
Axes of the slice: x: 4, y: 4, z: 8, core: 2. Of those that a mesh axis runs over, the one named last changes fastest.
Arguments:
- item_ids: int32 [262144], P('seq'), may hold values from 0 to 524287, as said below
- item_table: bfloat16 [524288, 512], P('seq', 'table'), may hold values from -6 to 6
- group_counts: int32 [16, 16, 16], replicated, may hold values from 0 to 96, as said below
- lengths: int32 [16], replicated, may hold values from 128 to 512
- history: bfloat16 [16, 2, 2, 512, 512], P('table', None, None, 'seq'), may hold values from -6 to 6
- w_in: bfloat16 [512, 2048], replicated, may hold values from -0.25 to 0.25
- w_out: bfloat16 [2048, 512], replicated, may hold values from -0.125 to 0.125
- w_proj: bfloat16 [2, 512, 1024], replicated, may hold values from -0.25 to 0.25
- w_back: bfloat16 [2, 512, 512], replicated, may hold values from -0.25 to 0.25
Outputs:
- ranked_states: bfloat16 [393216, 512], P(('table', 'seq'))
The draws below stay inside these ranges and needn't reach their ends.
Inputs may be any that keep to these rules, and one draw needn't show every extreme that they name: `item_ids`: the ids of the 16384 candidates of index s of seq lie in s * 32768 to (s + 1) * 32768 - 1. Each group_counts[t, s, :] sums to 1024; every sender has some entry equal to 96; on some index s every t sends 96 to one group.
All inputs are finite; a program needn't handle non-finite values.
Results may differ from the reference program's by a relative error of at most 0.013.
Values may be sent and summed in bfloat16 or wider, within the bound.
A program may use at most 128 MiB of HBM per device.

```python
import jax
import jax.numpy as jnp
from jax import lax

D = 512
FF = 2048
HEADS = 8
HEAD_DIM = 64
LAYERS = 2
HIST = 512
VOCAB_DEV = 32768
ROWS = 1024
GROUPS = 16
SHARDS = 16
CAP = 96
VOCAB = 524288
ROWS_SEQ = 16384
ROWS_ALL = 262144
SLOTS_ALL = 393216


def draw_item_ids(key, part):
    owner = jnp.arange(ROWS_ALL, dtype=jnp.int32) // ROWS_SEQ
    local_ids = jax.random.randint(key, (ROWS_ALL,), 0, VOCAB_DEV, dtype=jnp.int32)
    drawn = owner * VOCAB_DEV + local_ids
    return drawn.at[0].set(0).at[ROWS_ALL - 1].set(VOCAB - 1)


def draw_group_counts(key, part):
    pick_key, spot_key, walk_key = jax.random.split(jax.random.fold_in(key, 11), 3)
    senders = GROUPS * SHARDS
    full_at = jax.random.randint(pick_key, (GROUPS, SHARDS), 0, GROUPS, dtype=jnp.int32)
    spot_pair = jax.random.randint(spot_key, (2,), 0, GROUPS * SHARDS, dtype=jnp.int32)
    spot_group = spot_pair[0] % GROUPS
    spot_shard = spot_pair[1] % SHARDS
    full_at = jnp.where(jnp.arange(SHARDS, dtype=jnp.int32)[None, :] == spot_shard, spot_group, full_at).reshape(senders)
    columns = jnp.arange(GROUPS, dtype=jnp.int32)[None, :]
    position = jnp.where(columns < full_at[:, None], columns, columns - 1)
    remain = ROWS - CAP
    even_share = remain // (GROUPS - 1)
    leftover = remain - even_share * (GROUPS - 1)
    initial = jnp.where(columns == full_at[:, None], CAP, even_share + (position < leftover).astype(jnp.int32))
    steps_total = 4 * ROWS
    walk_pairs = jax.random.randint(walk_key, (steps_total, 2, senders), 0, GROUPS, dtype=jnp.int32)

    def walk_step(step_num, current):
        giver_col = walk_pairs[step_num, 0]
        taker_col = walk_pairs[step_num, 1]
        give_hot = (columns == giver_col[:, None]).astype(jnp.int32)
        take_hot = (columns == taker_col[:, None]).astype(jnp.int32)
        give_have = jnp.sum(current * give_hot, axis=1)
        take_have = jnp.sum(current * take_hot, axis=1)
        allowed = (giver_col != full_at) & (taker_col != full_at) & (giver_col != taker_col) & (give_have > 0) & (take_have < CAP)
        move_mask = allowed.astype(jnp.int32)[:, None]
        return current - move_mask * give_hot + move_mask * take_hot
    walked = lax.fori_loop(0, steps_total, walk_step, initial)
    return walked.reshape(GROUPS, SHARDS, GROUPS)


def draw_lengths(key, part):
    draw_key, pick_key = jax.random.split(jax.random.fold_in(key, 23), 2)
    drawn = jax.random.randint(draw_key, (GROUPS,), HIST // 4, HIST + 1, dtype=jnp.int32)
    picks = jax.random.randint(pick_key, (2,), 0, GROUPS, dtype=jnp.int32)
    longest = picks[0]
    shortest = (picks[0] + 1 + picks[1] % (GROUPS - 1)) % GROUPS
    return drawn.at[longest].set(HIST).at[shortest].set(HIST // 4)


def steps_of(stream_key, dims, cuts, least, top_value):
    gain = 1.0
    for axis_at, parts in cuts:
        heights = jax.random.uniform(jax.random.fold_in(jax.random.fold_in(stream_key, 6), axis_at), (parts,), jnp.float32, least / len(cuts), top_value / len(cuts))
        gain = gain * jnp.repeat(jnp.exp(heights), dims[axis_at] // parts).reshape((-1,) + (1,) * (len(dims) - 1 - axis_at))
    return gain


def bell_draw(stream_key, extent, deviation, bound, pieces=(), held_as=jnp.bfloat16):
    loudness = steps_of(stream_key, extent, pieces, -0.22, 0.18) if pieces else 1.0
    values = jax.random.normal(stream_key, extent, jnp.float32) * deviation * loudness
    return jnp.minimum(jnp.maximum(values, -bound), bound).astype(held_as)


def setup_inputs(seed: int = 0) -> dict:
    key_list = jax.random.split(jax.random.key(seed), 10)
    item_ids = draw_item_ids(jax.random.fold_in(key_list[9], 71), 0)
    item_table = bell_draw(key_list[1], (VOCAB, D), 1.0, 6.0, ((0, 16), (1, 16)))
    group_counts = draw_group_counts(jax.random.fold_in(key_list[9], 71), 0)
    lengths = draw_lengths(jax.random.fold_in(key_list[9], 71), 0)
    history = bell_draw(key_list[4], (GROUPS, LAYERS, 2, HIST, D), 1.0, 6.0, ((0, 16), (3, 16)))
    w_in = bell_draw(key_list[5], (D, FF), D ** -0.5, 0.25)
    w_out = bell_draw(key_list[6], (FF, D), FF ** -0.5, 0.125)
    w_proj = bell_draw(key_list[7], (LAYERS, D, 2 * D), D ** -0.5, 0.25)
    w_back = bell_draw(key_list[8], (LAYERS, D, D), D ** -0.5, 0.25)
    return dict(item_ids=item_ids, item_table=item_table, group_counts=group_counts, lengths=lengths, history=history, w_in=w_in, w_out=w_out, w_proj=w_proj, w_back=w_back)


def layer_norm(values):
    row_mean = lax.optimization_barrier(jnp.mean(values, axis=-1, keepdims=True))
    centred = values - row_mean
    variance = lax.optimization_barrier(jnp.mean(centred * centred, axis=-1, keepdims=True))
    return centred * lax.rsqrt(variance + 1e-06)

def stored(values):
    return lax.optimization_barrier(values.astype(jnp.bfloat16)).astype(jnp.float32)

def attend_layer(states, layer_cache, key_mask, w_proj, w_back):
    row_count = states.shape[0]
    normed = layer_norm(states.astype(jnp.float32)).astype(jnp.bfloat16)
    projected = jax.nn.silu(jnp.dot(normed, w_proj, preferred_element_type=jnp.float32))
    gate = projected[:, :D]
    queries = stored(projected[:, D:]).reshape(row_count, HEADS, HEAD_DIM)
    key_heads = layer_cache[0].astype(jnp.float32).reshape(HIST, HEADS, HEAD_DIM)
    value_heads = layer_cache[1].astype(jnp.float32).reshape(HIST, HEADS, HEAD_DIM)
    scores = jnp.einsum('qhd,khd->hqk', queries, key_heads) * HEAD_DIM ** (-0.5)
    weights = stored(jnp.where(key_mask[None, None, :], jax.nn.silu(scores), 0.0))
    attended = jnp.einsum('hqk,khd->qhd', weights, value_heads).reshape(row_count, D)
    mixed_rows = (layer_norm(attended) * gate).astype(jnp.bfloat16)
    return (states.astype(jnp.float32) + jnp.dot(mixed_rows, w_back, preferred_element_type=jnp.float32)).astype(jnp.bfloat16)

def reference(item_ids, item_table, group_counts, lengths, history, w_in, w_out, w_proj, w_back):
    embedded = jnp.take(item_table, item_ids, axis=0)
    hidden = jax.nn.silu(jnp.dot(embedded, w_in, preferred_element_type=jnp.float32)).astype(jnp.bfloat16)
    content = (embedded.astype(jnp.float32) + jnp.dot(hidden, w_out, preferred_element_type=jnp.float32)).astype(jnp.bfloat16)
    offsets = jnp.cumsum(group_counts, axis=2) - group_counts
    slot_ids = jnp.arange(CAP, dtype=jnp.int32)
    shard_ids = jnp.arange(SHARDS, dtype=jnp.int32)[:, None, None]
    table_ids = jnp.arange(GROUPS, dtype=jnp.int32)[None, :, None]

    def one_group(group_id):
        counts_here = group_counts[:, :, group_id].T
        offsets_here = offsets[:, :, group_id].T
        source = shard_ids * ROWS_SEQ + table_ids * ROWS + offsets_here[:, :, None] + slot_ids[None, None, :]
        source = jnp.minimum(source, ROWS_ALL - 1).astype(jnp.int32)
        filled = slot_ids[None, None, :] < counts_here[:, :, None]
        picked = jnp.take(content, source.reshape(-1), axis=0)
        states = jnp.where(filled.reshape(-1, 1), picked, jnp.zeros((), jnp.bfloat16))
        group_cache = history[group_id]
        key_mask = jnp.arange(HIST, dtype=jnp.int32) < lengths[group_id]

        def run_block(block_states):
            for layer_num in range(LAYERS):
                block_states = attend_layer(block_states, group_cache[layer_num], key_mask, w_proj[layer_num], w_back[layer_num])
            return block_states
        return lax.map(run_block, states.reshape(SHARDS, GROUPS * CAP, D))
    result = lax.map(one_group, jnp.arange(GROUPS, dtype=jnp.int32))
    return result.reshape(SLOTS_ALL, D)
```

```python
import functools

import jax
import jax.numpy as jnp
from jax import lax
from jax.experimental import pallas as pl
from jax.experimental.pallas import tpu as pltpu
from jax.sharding import Mesh
from jax.sharding import PartitionSpec as P

HEADS = 8
HEAD_DIM = 64
SEQ = ("seq_0", "seq_1")
TABLE_SEQ = ("table", "seq_0", "seq_1")
MESH = pl.DeviceIdType.MESH
CHUNKS = 4
UNROLL = 64
NT = (((1,), (1,)), ((), ()))


def table_steps(groups):
    chips = groups // 2
    order = [chips // 2]
    for far in range(chips // 2 - 1, 0, -1):
        order += [far, chips - far]
    order.append(0)
    return [(dz, dc) for dz in order for dc in (0, 1)][:-2] + [(0, 1), (0, 0)]


def identity(size_0, size_1, dtype):
    rows = lax.broadcasted_iota(jnp.int32, (size_0, size_1), 0)
    cols = lax.broadcasted_iota(jnp.int32, (size_0, size_1), 1)
    return (rows == cols).astype(dtype)


def exchange_kernel(
    dims,
    ids_ref,
    counts_ref,
    table_ref,
    hist_ref,
    emb_ref,
    cache_ref,
    wide,
    lanes_in,
    rows,
    window,
    outgoing,
    offsets,
    load_sem,
    piece_send,
    piece_recv,
    hist_send,
    hist_recv,
    own_sem,
):
    groups, seq_0, seq_1, vocab, columns, per_sender, cap, hist_rows = dims
    table_index = lax.axis_index("table")
    x = lax.axis_index("seq_0")
    y = lax.axis_index("seq_1")
    shard = x * seq_1 + y
    chips = groups // 2
    z = table_index // 2
    core = table_index % 2
    steps = table_steps(groups)
    hops = [(dx, dy) for dx in range(seq_0) for dy in range(seq_1) if (dx, dy) != (0, 0)]
    hops.sort(key=lambda d: -(min(d[0], seq_0 - d[0]) + min(d[1], seq_1 - d[1])))

    def table_peer(dz, dc):
        return ((z + dz) % chips) * 2 + (core + dc) % 2

    load = pltpu.make_async_copy(table_ref, lanes_in, load_sem)
    load.start()
    barrier = pltpu.get_barrier_semaphore()
    for dz, dc in steps[:-1]:
        pl.semaphore_signal(barrier, inc=1, device_id={"table": table_peer(dz, dc)}, device_id_type=MESH)
    for dx, dy in hops:
        pl.semaphore_signal(
            barrier,
            inc=1,
            device_id={"seq_0": (x + dx) % seq_0, "seq_1": (y + dy) % seq_1},
            device_id_type=MESH,
        )

    def offset_row(t, carry):
        total = jnp.int32(0)
        for g in range(groups):
            offsets[t, g] = total
            total = total + counts_ref[t, shard, g]
        return carry

    lax.fori_loop(0, groups, offset_row, 0)
    pl.semaphore_wait(barrier, len(steps) - 1 + len(hops))

    cache_here = cache_ref.at[:, :, pl.ds(shard * hist_rows, hist_rows), :]
    own_hist = pltpu.make_async_copy(hist_ref, cache_here, own_sem.at[CHUNKS])
    own_hist.start()
    hist_copies = []
    for n, (dx, dy) in enumerate(hops):
        copy = pltpu.make_async_remote_copy(
            src_ref=hist_ref,
            dst_ref=cache_here,
            send_sem=hist_send.at[n],
            recv_sem=hist_recv.at[n],
            device_id={"seq_0": (x + dx) % seq_0, "seq_1": (y + dy) % seq_1},
            device_id_type=MESH,
        )
        copy.start()
        hist_copies.append(copy)

    load.wait()
    block = 256
    eye = identity(block, block, jnp.bfloat16)
    blank = jnp.zeros((128 - columns, block), jnp.bfloat16)

    def widen(b, carry):
        at = pl.multiple_of(b * block, block)
        piece = jnp.concatenate([lanes_in[:, pl.ds(at, block)], blank], axis=0)
        wide[pl.ds(at, block), :] = lax.dot_general(eye, piece, NT, preferred_element_type=jnp.float32)
        return carry

    lax.fori_loop(0, vocab // block, widen, 0)

    senders = groups // CHUNKS
    chunk_rows = senders * per_sender
    chunk_slots = senders * cap
    fold = identity(columns, 128, jnp.bfloat16)
    slot_iota = lax.broadcasted_iota(jnp.int32, (cap, 128), 0)

    def piece_copy(j, n):
        dz, dc = steps[n]
        here = emb_ref.at[pl.ds(table_index * columns, columns), pl.ds(j * chunk_slots, chunk_slots)]
        if (dz, dc) == (0, 0):
            return pltpu.make_async_copy(outgoing.at[j, n], here, own_sem.at[j])
        return pltpu.make_async_remote_copy(
            src_ref=outgoing.at[j, n],
            dst_ref=here,
            send_sem=piece_send.at[j, n],
            recv_sem=piece_recv.at[j, n],
            device_id={"table": table_peer(dz, dc)},
            device_id_type=MESH,
        )

    def chunk(j, carry):
        def take(i, inner):
            base = i * UNROLL
            for u in range(UNROLL):
                item = ids_ref[j * chunk_rows + base + u] & (vocab - 1)
                rows[pl.ds(base + u, 1), :] = wide[pl.ds(item, 1), :]
            return inner

        lax.fori_loop(0, chunk_rows // UNROLL, take, 0)
        for n, (dz, dc) in enumerate(steps):
            g = table_peer(dz, dc)
            for t in range(senders):
                sender = j * senders + t
                start = offsets[sender, g]
                filled = counts_ref[sender, shard, g]
                taken = rows[pl.ds(start + t * per_sender, cap), :]
                window[n % 2, t * cap : (t + 1) * cap, :] = jnp.where(slot_iota < filled, taken, 0.0).astype(jnp.bfloat16)
            outgoing[j, n] = lax.dot_general(
                fold, window[n % 2], NT, preferred_element_type=jnp.float32
            ).astype(jnp.bfloat16)
            piece_copy(j, n).start()
        return carry

    lax.fori_loop(0, CHUNKS, chunk, 0)

    def finish(j, carry):
        for n in range(len(steps)):
            piece_copy(j, n).wait()
        return carry

    lax.fori_loop(0, CHUNKS, finish, 0)
    for copy in hist_copies:
        copy.wait()
    own_hist.wait()


def exchange(item_ids, item_table, group_counts, history):
    groups = lax.axis_size("table")
    seq_0, seq_1 = lax.axis_size("seq_0"), lax.axis_size("seq_1")
    vocab, columns = item_table.shape
    per_sender = item_ids.shape[0] // groups
    cap = 3 * per_sender // (2 * groups)
    layers, hist_rows, width = history.shape[1], history.shape[3], history.shape[4]
    slots = groups * cap
    senders = groups // CHUNKS
    dims = (groups, seq_0, seq_1, vocab, columns, per_sender, cap, hist_rows)
    return pl.pallas_call(
        functools.partial(exchange_kernel, dims),
        out_shape=(
            jax.ShapeDtypeStruct((groups * columns, slots), jnp.bfloat16),
            jax.ShapeDtypeStruct((layers, 2, hist_rows * seq_0 * seq_1, width), jnp.bfloat16),
        ),
        in_specs=[
            pl.BlockSpec(memory_space=pltpu.SMEM),
            pl.BlockSpec(memory_space=pltpu.SMEM),
            pl.BlockSpec(memory_space=pl.ANY),
            pl.BlockSpec(memory_space=pltpu.VMEM),
        ],
        out_specs=(pl.BlockSpec(memory_space=pl.ANY), pl.BlockSpec(memory_space=pl.ANY)),
        scratch_shapes=[
            pltpu.VMEM((vocab, 128), jnp.float32),
            pltpu.VMEM((columns, vocab), jnp.bfloat16),
            pltpu.VMEM((senders * per_sender + 128, 128), jnp.float32),
            pltpu.VMEM((2, senders * cap, 128), jnp.bfloat16),
            pltpu.VMEM((CHUNKS, groups, columns, senders * cap), jnp.bfloat16),
            pltpu.SMEM((groups, groups), jnp.int32),
            pltpu.SemaphoreType.DMA,
            pltpu.SemaphoreType.DMA((CHUNKS, groups)),
            pltpu.SemaphoreType.DMA((CHUNKS, groups)),
            pltpu.SemaphoreType.DMA((seq_0 * seq_1,)),
            pltpu.SemaphoreType.DMA((seq_0 * seq_1,)),
            pltpu.SemaphoreType.DMA((CHUNKS + 1,)),
        ],
        compiler_params=pltpu.CompilerParams(
            collective_id=0, has_side_effects=True, vmem_limit_bytes=60 * 1024 * 1024
        ),
        name="exchange",
    )(item_ids, group_counts, item_table.T, history[0])


def swish(half):
    return half + half * jnp.tanh(half)


def normalize(values):
    width = values.shape[-1]
    row_mean = jnp.sum(values, axis=-1, keepdims=True) * (1.0 / width)
    centred = values - row_mean
    variance = jnp.sum(centred * centred, axis=-1, keepdims=True) * (1.0 / width)
    return centred * lax.rsqrt(variance + 1e-06)


def rank_kernel(
    block,
    lengths_ref,
    emb_hbm,
    cache_hbm,
    w_in_hbm,
    w_out_hbm,
    w_proj_hbm,
    w_back_hbm,
    out_hbm,
    emb,
    cache,
    w_in,
    w_out,
    w_proj,
    w_back,
    keys,
    vals,
    hidden,
    weights,
    out,
    sems,
    out_sems,
):
    width, slots = emb.shape
    layers = w_proj.shape[0]
    hist = cache.shape[2]
    pairs = HEADS // 2
    pair_dim = 2 * HEAD_DIM
    sources = (emb_hbm, w_in_hbm, w_out_hbm, cache_hbm, w_proj_hbm, w_back_hbm)
    targets = (emb, w_in, w_out, cache, w_proj, w_back)
    loads = [pltpu.make_async_copy(s, d, sems.at[i]) for i, (s, d) in enumerate(zip(sources, targets))]
    for load in loads:
        load.start()
    group_length = lengths_ref[lax.axis_index("table")]
    for load in loads:
        load.wait()
    low = lax.broadcasted_iota(jnp.int32, (hist, pair_dim), 1) < HEAD_DIM
    live = lax.broadcasted_iota(jnp.int32, (hist, pair_dim), 0) < group_length
    zero = jnp.zeros((), jnp.bfloat16)
    for layer in range(layers):
        for p in range(pairs):
            cols = slice(p * pair_dim, (p + 1) * pair_dim)
            key = cache[layer, 0, :, cols]
            keys[layer, 2 * p] = jnp.where(low, key, zero)
            keys[layer, 2 * p + 1] = jnp.where(low, zero, key)
            val = jnp.where(live, cache[layer, 1, :, cols], zero)
            vals[layer, p, :hist] = jnp.where(low, val, zero)
            vals[layer, p, hist:] = jnp.where(low, zero, val)
    eye = identity(block, block, jnp.bfloat16)

    def dot(a, b):
        return jnp.dot(a, b, preferred_element_type=jnp.float32)

    def out_copy(i):
        return pltpu.make_async_copy(
            out.at[pl.ds(i * block, block), :], out_hbm.at[pl.ds(i * block, block), :], out_sems.at[i]
        )

    def run(i, carry):
        at = pl.multiple_of(i * block, block)
        rows = lax.dot_general(
            eye, emb[:, pl.ds(at, block)], NT, preferred_element_type=jnp.float32
        ).astype(jnp.bfloat16)
        ff = w_in.shape[1]
        step = 512
        for f in range(0, ff, step):
            hidden[:, f : f + step] = swish(dot(rows, w_in[:, f : f + step]) * 0.5).astype(jnp.bfloat16)
        states = (rows.astype(jnp.float32) + dot(hidden[...], w_out[...])).astype(jnp.bfloat16)
        for layer in range(layers):
            normed = normalize(states.astype(jnp.float32)).astype(jnp.bfloat16)
            gate = swish(dot(normed, w_proj[layer, :, :width]) * 0.5)
            query = swish(dot(normed, w_proj[layer, :, width:]) * 0.5).astype(jnp.bfloat16) * jnp.bfloat16(1 / 16)
            attended = []
            for p in range(pairs):
                query_pair = query[:, p * pair_dim : (p + 1) * pair_dim]
                for half in range(2):
                    score = lax.dot_general(
                        query_pair, keys[layer, 2 * p + half], NT, preferred_element_type=jnp.float32
                    )
                    weights[:, half * hist : (half + 1) * hist] = swish(score.astype(jnp.bfloat16))
                attended.append(dot(weights[...], vals[layer, p]))
            mixed = (normalize(jnp.concatenate(attended, axis=1)) * gate).astype(jnp.bfloat16)
            states = (states.astype(jnp.float32) + dot(mixed, w_back[layer])).astype(jnp.bfloat16)
        out[pl.ds(at, block), :] = states
        out_copy(i).start()
        return carry

    lax.fori_loop(0, slots // block, run, 0)

    def drain(i, carry):
        out_copy(i).wait()
        return carry

    lax.fori_loop(0, slots // block, drain, 0)


def rank(lengths, emb, cache, w_in, w_out, w_proj, w_back):
    width, slots = emb.shape
    layers = w_proj.shape[0]
    hist = cache.shape[2]
    block = slots // CHUNKS
    anywhere = pl.BlockSpec(memory_space=pl.ANY)
    return pl.pallas_call(
        functools.partial(rank_kernel, block),
        out_shape=jax.ShapeDtypeStruct((slots, width), jnp.bfloat16),
        in_specs=[pl.BlockSpec(memory_space=pltpu.SMEM)] + [anywhere] * 6,
        out_specs=anywhere,
        scratch_shapes=[
            pltpu.VMEM(a.shape, a.dtype) for a in (emb, cache, w_in, w_out, w_proj, w_back)
        ]
        + [
            pltpu.VMEM((layers, HEADS, hist, 2 * HEAD_DIM), jnp.bfloat16),
            pltpu.VMEM((layers, HEADS // 2, 2 * hist, 2 * HEAD_DIM), jnp.bfloat16),
            pltpu.VMEM((block, w_in.shape[1]), jnp.bfloat16),
            pltpu.VMEM((block, 2 * hist), jnp.bfloat16),
            pltpu.VMEM((slots, width), jnp.bfloat16),
            pltpu.SemaphoreType.DMA((6,)),
            pltpu.SemaphoreType.DMA((slots // block,)),
        ],
        compiler_params=pltpu.CompilerParams(vmem_limit_bytes=60 * 1024 * 1024),
        name="rank",
    )(lengths, emb, cache, w_in, w_out, w_proj, w_back)


def local(item_ids, item_table, group_counts, lengths, history, w_in, w_out, w_proj, w_back):
    emb, cache = exchange(item_ids, item_table, group_counts, history)
    return rank(lengths, emb, cache, w_in, w_out, w_proj, w_back)


def solution(mesh):
    torus = Mesh(mesh.devices.reshape(mesh.shape["table"], 4, 4), ("table", "seq_0", "seq_1"))
    in_specs = (
        P(SEQ),
        P(SEQ, "table"),
        P(),
        P(),
        P("table", None, None, SEQ, None),
        P(),
        P(),
        P(),
        P(),
    )
    out_specs = P(TABLE_SEQ, None)
    return jax.shard_map(local, mesh=torus, in_specs=in_specs, out_specs=out_specs, check_vma=False)
```

```python
import functools

import jax
import jax.numpy as jnp
from jax import lax
from jax.experimental import pallas as pl
from jax.experimental.pallas import tpu as pltpu
from jax.sharding import Mesh
from jax.sharding import PartitionSpec as P

HEADS = 8
HEAD_DIM = 64
SEQ = ("seq_0", "seq_1")
TABLE_SEQ = ("table", "seq_0", "seq_1")
MESH = pl.DeviceIdType.MESH
CHUNKS = 4
NT = (((1,), (1,)), ((), ()))


def table_steps(groups):
    chips = groups // 2
    order = [chips // 2]
    for far in range(chips // 2 - 1, 0, -1):
        order += [far, chips - far]
    order.append(0)
    return [(dz, dc) for dz in order for dc in (0, 1)][:-2] + [(0, 1), (0, 0)]


def identity(size_0, size_1, dtype):
    rows = lax.broadcasted_iota(jnp.int32, (size_0, size_1), 0)
    cols = lax.broadcasted_iota(jnp.int32, (size_0, size_1), 1)
    return (rows == cols).astype(dtype)


def swish(half):
    return half + half * jnp.tanh(half)


def normalize(values):
    width = values.shape[-1]
    row_mean = jnp.sum(values, axis=-1, keepdims=True) * (1.0 / width)
    centred = values - row_mean
    variance = jnp.sum(centred * centred, axis=-1, keepdims=True) * (1.0 / width)
    return centred * lax.rsqrt(variance + 1e-06)


def dot(a, b):
    return jnp.dot(a, b, preferred_element_type=jnp.float32)


def dot_nt(a, b):
    return lax.dot_general(a, b, NT, preferred_element_type=jnp.float32)


def build_caches(cache, keys, vals, group_length):
    layers, _, hist, _ = cache.shape
    pair_dim = 2 * HEAD_DIM
    low = lax.broadcasted_iota(jnp.int32, (hist, pair_dim), 1) < HEAD_DIM
    live = lax.broadcasted_iota(jnp.int32, (hist, pair_dim), 0) < group_length
    zero = jnp.zeros((), jnp.bfloat16)
    for layer in range(layers):
        for p in range(HEADS // 2):
            cols = slice(p * pair_dim, (p + 1) * pair_dim)
            key = cache[layer, 0, :, cols]
            keys[layer, 2 * p] = jnp.where(low, key, zero)
            keys[layer, 2 * p + 1] = jnp.where(low, zero, key)
            val = jnp.where(live, cache[layer, 1, :, cols], zero)
            vals[layer, p, :hist] = jnp.where(low, val, zero)
            vals[layer, p, hist:] = jnp.where(low, zero, val)


def rank_block(rows, w_in, w_out, w_proj, w_back, keys, vals, hidden, weights):
    width = rows.shape[1]
    ff = w_in.shape[1]
    hist = keys.shape[2]
    pair_dim = 2 * HEAD_DIM
    half = jnp.bfloat16(0.5)
    step = 512
    half_rows = rows * half
    for f in range(0, ff, step):
        hidden[:, f : f + step] = swish(dot(half_rows, w_in[:, f : f + step]).astype(jnp.bfloat16))
    states = (rows.astype(jnp.float32) + dot(hidden[...], w_out[...])).astype(jnp.bfloat16)
    for layer in range(w_proj.shape[0]):
        normed = normalize(states.astype(jnp.float32)).astype(jnp.bfloat16) * half
        query = swish(dot(normed, w_proj[layer, :, width:])).astype(jnp.bfloat16) * jnp.bfloat16(1 / 16)
        gate = swish(dot(normed, w_proj[layer, :, :width]))
        attended = []
        for p in range(HEADS // 2):
            query_pair = query[:, p * pair_dim : (p + 1) * pair_dim]
            for part in range(2):
                score = dot_nt(query_pair, keys[layer, 2 * p + part])
                weights[:, part * hist : (part + 1) * hist] = swish(score.astype(jnp.bfloat16))
            attended.append(dot(weights[...], vals[layer, p]))
        mixed = (normalize(jnp.concatenate(attended, axis=1)) * gate).astype(jnp.bfloat16)
        states = (states.astype(jnp.float32) + dot(mixed, w_back[layer])).astype(jnp.bfloat16)
    return states


def rank_kernel(
    dims,
    lengths_ref,
    ids_hbm,
    counts_hbm,
    table_hbm,
    hist_hbm,
    w_in_hbm,
    w_out_hbm,
    w_proj_hbm,
    w_back_hbm,
    out_hbm,
    wide,
    lanes_in,
    ids_in,
    ids_low,
    ids,
    counts,
    offsets,
    rows,
    window,
    outgoing,
    emb,
    cache,
    w_in,
    w_out,
    w_proj,
    w_back,
    keys,
    vals,
    hidden,
    weights,
    out,
    load_sem,
    weight_sem,
    piece_send,
    piece_recv,
    hist_send,
    hist_recv,
    own_sem,
    out_sem,
):
    groups, seq_0, seq_1, vocab, columns, per_sender, cap, hist_rows = dims
    table_index = lax.axis_index("table")
    x = lax.axis_index("seq_0")
    y = lax.axis_index("seq_1")
    shard = x * seq_1 + y
    chips = groups // 2
    z = table_index // 2
    core = table_index % 2
    steps = table_steps(groups)
    hops = [(dx, dy) for dx in range(seq_0) for dy in range(seq_1) if (dx, dy) != (0, 0)]
    hops.sort(key=lambda d: -(min(d[0], seq_0 - d[0]) + min(d[1], seq_1 - d[1])))
    senders = groups // CHUNKS
    chunk_rows = senders * per_sender
    chunk_slots = senders * cap

    def table_peer(dz, dc):
        return ((z + dz) % chips) * 2 + (core + dc) % 2

    cache_here = cache.at[:, :, pl.ds(shard * hist_rows, hist_rows), :]
    load_ids = pltpu.make_async_copy(ids_hbm, ids_in, load_sem.at[0])
    load_table = pltpu.make_async_copy(table_hbm, lanes_in, load_sem.at[1])
    load_counts = pltpu.make_async_copy(counts_hbm.at[:, shard, :], counts, load_sem.at[2])
    load_hist = pltpu.make_async_copy(hist_hbm, cache_here, load_sem.at[3])
    for load in (load_ids, load_table, load_counts, load_hist):
        load.start()
    sources = (w_in_hbm, w_out_hbm, w_proj_hbm, w_back_hbm)
    targets = (w_in, w_out, w_proj, w_back)
    weight_loads = [pltpu.make_async_copy(s, d, weight_sem.at[i]) for i, (s, d) in enumerate(zip(sources, targets))]
    for load in weight_loads:
        load.start()

    barrier = pltpu.get_barrier_semaphore()
    for dz, dc in steps[:-1]:
        pl.semaphore_signal(barrier, inc=1, device_id={"table": table_peer(dz, dc)}, device_id_type=MESH)
    for dx, dy in hops:
        pl.semaphore_signal(
            barrier,
            inc=1,
            device_id={"seq_0": (x + dx) % seq_0, "seq_1": (y + dy) % seq_1},
            device_id_type=MESH,
        )

    load_ids.wait()
    ids_low[...] = ids_in[...] & (vocab - 1)
    move_ids = pltpu.make_async_copy(ids_low, ids, load_sem.at[0])
    move_ids.start()
    load_table.wait()
    block = 256
    eye = identity(block, block, jnp.bfloat16)
    blank = jnp.zeros((128 - columns, block), jnp.bfloat16)

    def widen(b, carry):
        at = pl.multiple_of(b * 2 * block, 2 * block)
        piece = jnp.concatenate(
            [lanes_in[:, pl.ds(at, block)], blank, lanes_in[:, pl.ds(at + block, block)], blank], axis=0
        )
        turned = dot_nt(eye, piece)
        wide[pl.ds(at, block), :] = turned[:, :128]
        wide[pl.ds(at + block, block), :] = turned[:, 128:]
        return carry

    lax.fori_loop(0, vocab // (2 * block), widen, 0)

    load_counts.wait()

    def offset_row(t, carry):
        total = jnp.int32(0)
        for g in range(groups):
            offsets[t, g] = total
            total = total + counts[t, g]
        return carry

    lax.fori_loop(0, groups, offset_row, 0)
    load_hist.wait()
    pl.semaphore_wait(barrier, len(steps) - 1 + len(hops))

    hist_copies = []
    for n, (dx, dy) in enumerate(hops):
        copy = pltpu.make_async_remote_copy(
            src_ref=cache_here,
            dst_ref=cache_here,
            send_sem=hist_send.at[n],
            recv_sem=hist_recv.at[n],
            device_id={"seq_0": (x + dx) % seq_0, "seq_1": (y + dy) % seq_1},
            device_id_type=MESH,
        )
        copy.start()
        hist_copies.append(copy)

    fold = identity(columns, 128, jnp.bfloat16)
    slot_iota = lax.broadcasted_iota(jnp.int32, (cap, 128), 0)

    def own_copy(j):
        here = emb.at[pl.ds(table_index * columns, columns), pl.ds(j * chunk_slots, chunk_slots)]
        return pltpu.make_async_copy(outgoing.at[j, len(steps) - 1], here, own_sem.at[j])

    def piece_copy(j, n):
        dz, dc = steps[n]
        return pltpu.make_async_remote_copy(
            src_ref=outgoing.at[j, n],
            dst_ref=emb.at[pl.ds(table_index * columns, columns), pl.ds(j * chunk_slots, chunk_slots)],
            send_sem=piece_send.at[j, n],
            recv_sem=piece_recv.at[j, n],
            device_id={"table": table_peer(dz, dc)},
            device_id_type=MESH,
        )

    move_ids.wait()
    id_rows = chunk_rows // 128

    def chunk(j, carry):
        def take(i, inner):
            id_row = j * id_rows + i
            base = pl.multiple_of(i * 128, 128)
            for u in range(128):
                rows[pl.ds(base + u, 1), :] = wide[pl.ds(ids[id_row, u], 1), :]
            return inner

        lax.fori_loop(0, id_rows, take, 0)
        for n, (dz, dc) in enumerate(steps):
            g = table_peer(dz, dc)
            for t in range(senders):
                sender = j * senders + t
                start = offsets[sender, g]
                filled = counts[sender, g]
                taken = rows[pl.ds(start + t * per_sender, cap), :]
                window[n % 2, t * cap : (t + 1) * cap, :] = jnp.where(slot_iota < filled, taken, 0.0).astype(jnp.bfloat16)
            outgoing[j, n] = dot_nt(fold, window[n % 2]).astype(jnp.bfloat16)
            if n < len(steps) - 1:
                piece_copy(j, n).start()
            else:
                own_copy(j).start()
        return carry

    lax.fori_loop(0, CHUNKS, chunk, 0)

    for load in weight_loads:
        load.wait()
    for copy in hist_copies:
        copy.wait()
    build_caches(cache, keys, vals, lengths_ref[table_index])
    turn = identity(chunk_slots, chunk_slots, jnp.bfloat16)

    def out_copy(j):
        here = pl.ds(pl.multiple_of(j * chunk_slots, chunk_slots), chunk_slots)
        return pltpu.make_async_copy(out.at[here, :], out_hbm.at[here, :], out_sem.at[j])

    def run(j, carry):
        for n in range(len(steps) - 1):
            piece_copy(j, n).wait()
        own_copy(j).wait()
        at = pl.multiple_of(j * chunk_slots, chunk_slots)
        content_in = dot_nt(turn, emb[:, pl.ds(at, chunk_slots)]).astype(jnp.bfloat16)
        out[pl.ds(at, chunk_slots), :] = rank_block(
            content_in, w_in, w_out, w_proj, w_back, keys, vals, hidden, weights
        )
        out_copy(j).start()
        return carry

    lax.fori_loop(0, CHUNKS, run, 0)

    def drain(j, carry):
        out_copy(j).wait()
        return carry

    lax.fori_loop(0, CHUNKS, drain, 0)


def local(item_ids, item_table, group_counts, lengths, history, w_in, w_out, w_proj, w_back):
    groups = lax.axis_size("table")
    seq_0, seq_1 = lax.axis_size("seq_0"), lax.axis_size("seq_1")
    vocab, columns = item_table.shape
    per_sender = item_ids.shape[0] // groups
    cap = 3 * per_sender // (2 * groups)
    layers, hist_rows, width = history.shape[1], history.shape[3], history.shape[4]
    hist = hist_rows * seq_0 * seq_1
    slots = groups * cap
    senders = groups // CHUNKS
    block = senders * cap
    dims = (groups, seq_0, seq_1, vocab, columns, per_sender, cap, hist_rows)
    id_rows = item_ids.shape[0] // 128
    anywhere = pl.BlockSpec(memory_space=pl.ANY)
    vmem, dma = pltpu.VMEM, pltpu.SemaphoreType.DMA
    return pl.pallas_call(
        functools.partial(rank_kernel, dims),
        out_shape=jax.ShapeDtypeStruct((slots, width), jnp.bfloat16),
        in_specs=[pl.BlockSpec(memory_space=pltpu.SMEM)] + [anywhere] * 8,
        out_specs=anywhere,
        scratch_shapes=[
            vmem((vocab, 128), jnp.float32),
            vmem((columns, vocab), jnp.bfloat16),
            vmem((id_rows, 128), jnp.int32),
            vmem((id_rows, 128), jnp.int32),
            pltpu.SMEM((id_rows, 128), jnp.int32),
            pltpu.SMEM((groups, groups), jnp.int32),
            pltpu.SMEM((groups, groups), jnp.int32),
            vmem((senders * per_sender + 128, 128), jnp.float32),
            vmem((2, block, 128), jnp.bfloat16),
            vmem((CHUNKS, groups, columns, block), jnp.bfloat16),
            vmem((width, slots), jnp.bfloat16),
            vmem((layers, 2, hist, width), jnp.bfloat16),
            vmem(w_in.shape, jnp.bfloat16),
            vmem(w_out.shape, jnp.bfloat16),
            vmem(w_proj.shape, jnp.bfloat16),
            vmem(w_back.shape, jnp.bfloat16),
            vmem((layers, HEADS, hist, 2 * HEAD_DIM), jnp.bfloat16),
            vmem((layers, HEADS // 2, 2 * hist, 2 * HEAD_DIM), jnp.bfloat16),
            vmem((block, w_in.shape[1]), jnp.bfloat16),
            vmem((block, 2 * hist), jnp.bfloat16),
            vmem((slots, width), jnp.bfloat16),
            dma((4,)),
            dma((4,)),
            dma((CHUNKS, groups)),
            dma((CHUNKS, groups)),
            dma((seq_0 * seq_1,)),
            dma((seq_0 * seq_1,)),
            dma((CHUNKS,)),
            dma((CHUNKS,)),
        ],
        compiler_params=pltpu.CompilerParams(
            collective_id=0, has_side_effects=True, vmem_limit_bytes=62 * 1024 * 1024
        ),
        name="rank",
    )(lengths, item_ids.reshape(id_rows, 128), group_counts, item_table.T, history[0], w_in, w_out, w_proj, w_back)


def solution(mesh):
    torus = Mesh(mesh.devices.reshape(mesh.shape["table"], 4, 4), ("table", "seq_0", "seq_1"))
    in_specs = (
        P(SEQ),
        P(SEQ, "table"),
        P(),
        P(),
        P("table", None, None, SEQ, None),
        P(),
        P(),
        P(),
        P(),
    )
    out_specs = P(TABLE_SEQ, None)
    return jax.shard_map(local, mesh=torus, in_specs=in_specs, out_specs=out_specs, check_vma=False)
```

```python
import functools

import jax
import jax.numpy as jnp
from jax import lax
from jax.experimental import pallas as pl
from jax.experimental.pallas import tpu as pltpu
from jax.sharding import Mesh
from jax.sharding import PartitionSpec as P

HEADS = 8
HEAD_DIM = 64
SEQ = ("seq_0", "seq_1")
TABLE_SEQ = ("table", "seq_0", "seq_1")
MESH = pl.DeviceIdType.MESH
CHUNKS = 4
TAKE = 8
NT = (((1,), (1,)), ((), ()))


def table_steps(groups):
    chips = groups // 2
    order = [chips // 2]
    for far in range(chips // 2 - 1, 0, -1):
        order += [far, chips - far]
    order.append(0)
    return [(dz, dc) for dz in order for dc in (0, 1)][:-2] + [(0, 1), (0, 0)]


def identity(size_0, size_1, dtype):
    rows = lax.broadcasted_iota(jnp.int32, (size_0, size_1), 0)
    cols = lax.broadcasted_iota(jnp.int32, (size_0, size_1), 1)
    return (rows == cols).astype(dtype)


def swish(half):
    return half + half * jnp.tanh(half)


def normalize(values):
    width = values.shape[-1]
    row_mean = jnp.sum(values, axis=-1, keepdims=True) * (1.0 / width)
    centred = values - row_mean
    variance = jnp.sum(centred * centred, axis=-1, keepdims=True) * (1.0 / width)
    return centred * lax.rsqrt(variance + 1e-06)


def dot(a, b):
    return jnp.dot(a, b, preferred_element_type=jnp.float32)


def dot_nt(a, b):
    return lax.dot_general(a, b, NT, preferred_element_type=jnp.float32)


def build_caches(cache, keys, vals, group_length):
    layers, _, seq_0, part, _ = cache.shape
    hist = seq_0 * part
    pair_dim = 2 * HEAD_DIM
    low = lax.broadcasted_iota(jnp.int32, (hist, pair_dim), 1) < HEAD_DIM
    live = lax.broadcasted_iota(jnp.int32, (hist, pair_dim), 0) < group_length
    zero = jnp.zeros((), jnp.bfloat16)
    for layer in range(layers):
        for p in range(HEADS // 2):
            cols = slice(p * pair_dim, (p + 1) * pair_dim)
            key = cache[layer, 0, :, :, cols].reshape(hist, pair_dim)
            keys[layer, 2 * p] = jnp.where(low, key, zero)
            keys[layer, 2 * p + 1] = jnp.where(low, zero, key)
            val = jnp.where(live, cache[layer, 1, :, :, cols].reshape(hist, pair_dim), zero)
            vals[layer, p, :hist] = jnp.where(low, val, zero)
            vals[layer, p, hist:] = jnp.where(low, zero, val)


def rank_block(rows, w_in, w_out, w_proj, w_back, keys, vals, hidden, weights):
    width = rows.shape[1]
    ff = w_in.shape[1]
    hist = keys.shape[2]
    pair_dim = 2 * HEAD_DIM
    half = jnp.bfloat16(0.5)
    step = 512
    half_rows = rows * half
    for f in range(0, ff, step):
        hidden[:, f : f + step] = swish(dot(half_rows, w_in[:, f : f + step]).astype(jnp.bfloat16))
    states = (rows.astype(jnp.float32) + dot(hidden[...], w_out[...])).astype(jnp.bfloat16)
    for layer in range(w_proj.shape[0]):
        normed = normalize(states.astype(jnp.float32)).astype(jnp.bfloat16) * half
        query = swish(dot(normed, w_proj[layer, :, width:])).astype(jnp.bfloat16) * jnp.bfloat16(1 / 16)
        gate = swish(dot(normed, w_proj[layer, :, :width]))
        attended = []
        for p in range(HEADS // 2):
            query_pair = query[:, p * pair_dim : (p + 1) * pair_dim]
            for part in range(2):
                score = dot_nt(query_pair, keys[layer, 2 * p + part])
                weights[:, part * hist : (part + 1) * hist] = swish(score.astype(jnp.bfloat16))
            attended.append(dot(weights[...], vals[layer, p]))
        mixed = (normalize(jnp.concatenate(attended, axis=1)) * gate).astype(jnp.bfloat16)
        states = (states.astype(jnp.float32) + dot(mixed, w_back[layer])).astype(jnp.bfloat16)
    return states


def rank_kernel(
    dims,
    lengths_hbm,
    ids_hbm,
    counts_hbm,
    table_hbm,
    hist_hbm,
    w_in_hbm,
    w_out_hbm,
    w_proj_hbm,
    w_back_hbm,
    out,
    wide,
    lanes_in,
    ids_in,
    ids_low,
    ids,
    counts,
    lengths,
    offsets,
    rows,
    window,
    outgoing,
    emb,
    cache,
    w_in,
    w_out,
    w_proj,
    w_back,
    keys,
    vals,
    hidden,
    weights,
    load_sem,
    weight_sem,
    piece_send,
    piece_recv,
    hist_send,
    hist_recv,
    own_sem,
):
    groups, seq_0, seq_1, vocab, columns, per_sender, cap, hist_rows = dims
    table_index = lax.axis_index("table")
    x = lax.axis_index("seq_0")
    y = lax.axis_index("seq_1")
    shard = x * seq_1 + y
    chips = groups // 2
    z = table_index // 2
    core = table_index % 2
    steps = table_steps(groups)
    x_far = sorted(range(1, seq_0), key=lambda d: -min(d, seq_0 - d))
    y_far = sorted(range(1, seq_1), key=lambda d: -min(d, seq_1 - d))
    senders = groups // CHUNKS
    chunk_rows = senders * per_sender
    chunk_slots = senders * cap

    def table_peer(dz, dc):
        return ((z + dz) % chips) * 2 + (core + dc) % 2

    mine = pl.ds(y * hist_rows, hist_rows)
    load_ids = pltpu.make_async_copy(ids_hbm, ids_in, load_sem.at[0])
    load_table = pltpu.make_async_copy(table_hbm, lanes_in, load_sem.at[1])
    load_counts = pltpu.make_async_copy(counts_hbm.at[:, shard, :], counts, load_sem.at[2])
    load_hist = pltpu.make_async_copy(hist_hbm, cache.at[:, :, x, mine, :], load_sem.at[3])
    load_lengths = pltpu.make_async_copy(lengths_hbm, lengths, load_sem.at[4])
    for load in (load_ids, load_table, load_counts, load_hist, load_lengths):
        load.start()
    sources = (w_in_hbm, w_out_hbm, w_proj_hbm, w_back_hbm)
    targets = (w_in, w_out, w_proj, w_back)
    weight_loads = [pltpu.make_async_copy(s, d, weight_sem.at[i]) for i, (s, d) in enumerate(zip(sources, targets))]

    barrier = pltpu.get_barrier_semaphore()
    for dz, dc in steps[:-1]:
        pl.semaphore_signal(barrier, inc=1, device_id={"table": table_peer(dz, dc)}, device_id_type=MESH)
    for d in x_far:
        pl.semaphore_signal(barrier, inc=1, device_id={"seq_0": (x + d) % seq_0}, device_id_type=MESH)
    for d in y_far:
        pl.semaphore_signal(barrier, inc=1, device_id={"seq_1": (y + d) % seq_1}, device_id_type=MESH)

    load_ids.wait()
    ids_low[...] = ids_in[...] & (vocab - 1)
    move_ids = pltpu.make_async_copy(ids_low, ids, load_sem.at[0])
    move_ids.start()
    load_table.wait()
    for load in weight_loads:
        load.start()
    block = 256
    eye = identity(block, block, jnp.bfloat16)
    blank = jnp.zeros((128 - columns, block), jnp.bfloat16)

    def widen(b, carry):
        at = pl.multiple_of(b * 2 * block, 2 * block)
        piece = jnp.concatenate(
            [lanes_in[:, pl.ds(at, block)], blank, lanes_in[:, pl.ds(at + block, block)], blank], axis=0
        )
        turned = dot_nt(eye, piece)
        wide[pl.ds(at, block), :] = turned[:, :128]
        wide[pl.ds(at + block, block), :] = turned[:, 128:]
        return carry

    lax.fori_loop(0, vocab // (2 * block), widen, 0)

    load_counts.wait()
    load_lengths.wait()

    def offset_row(t, carry):
        total = jnp.int32(0)
        for g in range(groups):
            offsets[t, g] = total
            total = total + counts[t, g]
        return carry

    lax.fori_loop(0, groups, offset_row, 0)
    load_hist.wait()
    pl.semaphore_wait(barrier, len(steps) - 1 + len(x_far) + len(y_far))

    def hist_copy(n, view, axis, to):
        return pltpu.make_async_remote_copy(
            src_ref=view,
            dst_ref=view,
            send_sem=hist_send.at[n],
            recv_sem=hist_recv.at[n],
            device_id={axis: to},
            device_id_type=MESH,
        )

    own_keys = cache.at[:, 0, x, mine, :]
    own_vals = cache.at[:, 1, x, mine, :]
    row_keys = cache.at[:, 0, x, :, :]
    row_vals = cache.at[:, 1, :, mine, :]
    first, second = [], []
    for d in y_far:
        first.append(hist_copy(len(first), own_keys, "seq_1", (y + d) % seq_1))
    for d in x_far:
        first.append(hist_copy(len(first), own_vals, "seq_0", (x + d) % seq_0))
    for d in x_far:
        second.append(hist_copy(len(first) + len(second), row_keys, "seq_0", (x + d) % seq_0))
    for d in y_far:
        second.append(hist_copy(len(first) + len(second), row_vals, "seq_1", (y + d) % seq_1))
    for copy in first:
        copy.start()

    fold = identity(columns, 128, jnp.bfloat16)
    slot_iota = lax.broadcasted_iota(jnp.int32, (cap, 128), 0)

    def own_copy(j):
        here = emb.at[pl.ds(table_index * columns, columns), pl.ds(j * chunk_slots, chunk_slots)]
        return pltpu.make_async_copy(outgoing.at[j, len(steps) - 1], here, own_sem.at[j])

    def piece_copy(j, n):
        dz, dc = steps[n]
        return pltpu.make_async_remote_copy(
            src_ref=outgoing.at[j, n],
            dst_ref=emb.at[pl.ds(table_index * columns, columns), pl.ds(j * chunk_slots, chunk_slots)],
            send_sem=piece_send.at[j, n],
            recv_sem=piece_recv.at[j, n],
            device_id={"table": table_peer(dz, dc)},
            device_id_type=MESH,
        )

    move_ids.wait()
    id_rows = chunk_rows // 128
    places = [table_index // groups + u for u in range(TAKE)]

    def chunk(j, carry):
        def take(i, inner):
            for v in range(128 // TAKE):
                some = ids.at[j * id_rows + i, pl.ds(v * TAKE, TAKE)]
                into = rows.at[pl.ds(pl.multiple_of(i * 128 + v * TAKE, TAKE), TAKE), :]
                for u in range(TAKE):
                    into[u : u + 1, :] = wide[pl.ds(some[places[u]], 1), :]
            return inner

        lax.fori_loop(0, id_rows, take, 0)
        for n, (dz, dc) in enumerate(steps):
            g = table_peer(dz, dc)
            for t in range(senders):
                sender = j * senders + t
                start = offsets[sender, g]
                filled = counts[sender, g]
                taken = rows[pl.ds(start + t * per_sender, cap), :]
                window[n % 2, t * cap : (t + 1) * cap, :] = jnp.where(slot_iota < filled, taken, 0.0).astype(jnp.bfloat16)
            outgoing[j, n] = dot_nt(fold, window[n % 2]).astype(jnp.bfloat16)
            if n < len(steps) - 1:
                piece_copy(j, n).start()
            else:
                own_copy(j).start()

        @pl.when(j == 0)
        def _():
            for copy in first:
                copy.wait()
            for copy in second:
                copy.start()

        return carry

    lax.fori_loop(0, CHUNKS, chunk, 0)

    for load in weight_loads:
        load.wait()
    for copy in second:
        copy.wait()
    build_caches(cache, keys, vals, lengths[table_index])
    turn = identity(chunk_slots, chunk_slots, jnp.bfloat16)

    def run(j, carry):
        for n in range(len(steps) - 1):
            piece_copy(j, n).wait()
        own_copy(j).wait()
        at = pl.multiple_of(j * chunk_slots, chunk_slots)
        content_in = dot_nt(turn, emb[:, pl.ds(at, chunk_slots)]).astype(jnp.bfloat16)
        out[pl.ds(at, chunk_slots), :] = rank_block(
            content_in, w_in, w_out, w_proj, w_back, keys, vals, hidden, weights
        )
        return carry

    lax.fori_loop(0, CHUNKS, run, 0)


def local(item_ids, item_table, group_counts, lengths, history, w_in, w_out, w_proj, w_back):
    groups = lax.axis_size("table")
    seq_0, seq_1 = lax.axis_size("seq_0"), lax.axis_size("seq_1")
    vocab, columns = item_table.shape
    per_sender = item_ids.shape[0] // groups
    cap = 3 * per_sender // (2 * groups)
    layers, hist_rows, width = history.shape[1], history.shape[3], history.shape[4]
    hist = hist_rows * seq_0 * seq_1
    slots = groups * cap
    senders = groups // CHUNKS
    block = senders * cap
    dims = (groups, seq_0, seq_1, vocab, columns, per_sender, cap, hist_rows)
    id_rows = item_ids.shape[0] // 128
    in_hbm = pl.BlockSpec(memory_space=pltpu.HBM)
    vmem, dma = pltpu.VMEM, pltpu.SemaphoreType.DMA
    operands = (lengths, item_ids.reshape(id_rows, 128), group_counts, item_table.T, history[0], w_in, w_out, w_proj, w_back)
    operands = [pltpu.with_memory_space_constraint(a, pltpu.HBM) for a in operands]
    return pl.pallas_call(
        functools.partial(rank_kernel, dims),
        out_shape=jax.ShapeDtypeStruct((slots, width), jnp.bfloat16),
        in_specs=[in_hbm] * 9,
        out_specs=pl.BlockSpec(memory_space=pltpu.VMEM),
        scratch_shapes=[
            vmem((vocab, 128), jnp.float32),
            vmem((columns, vocab), jnp.bfloat16),
            vmem((id_rows, 128), jnp.int32),
            vmem((id_rows, 128), jnp.int32),
            pltpu.SMEM((id_rows, 128), jnp.int32),
            pltpu.SMEM((groups, groups), jnp.int32),
            pltpu.SMEM((groups,), jnp.int32),
            pltpu.SMEM((groups, groups), jnp.int32),
            vmem((senders * per_sender + 128, 128), jnp.float32),
            vmem((2, block, 128), jnp.bfloat16),
            vmem((CHUNKS, groups, columns, block), jnp.bfloat16),
            vmem((width, slots), jnp.bfloat16),
            vmem((layers, 2, seq_0, seq_1 * hist_rows, width), jnp.bfloat16),
            vmem(w_in.shape, jnp.bfloat16),
            vmem(w_out.shape, jnp.bfloat16),
            vmem(w_proj.shape, jnp.bfloat16),
            vmem(w_back.shape, jnp.bfloat16),
            vmem((layers, HEADS, hist, 2 * HEAD_DIM), jnp.bfloat16),
            vmem((layers, HEADS // 2, 2 * hist, 2 * HEAD_DIM), jnp.bfloat16),
            vmem((block, w_in.shape[1]), jnp.bfloat16),
            vmem((block, 2 * hist), jnp.bfloat16),
            dma((5,)),
            dma((4,)),
            dma((CHUNKS, groups)),
            dma((CHUNKS, groups)),
            dma((2 * (seq_0 + seq_1 - 2),)),
            dma((2 * (seq_0 + seq_1 - 2),)),
            dma((CHUNKS,)),
        ],
        compiler_params=pltpu.CompilerParams(
            collective_id=0, has_side_effects=True, vmem_limit_bytes=50 * 1024 * 1024
        ),
        name="rank",
    )(*operands)


def solution(mesh):
    torus = Mesh(mesh.devices.reshape(mesh.shape["table"], 4, 4), ("table", "seq_0", "seq_1"))
    in_specs = (
        P(SEQ),
        P(SEQ, "table"),
        P(),
        P(),
        P("table", None, None, SEQ, None),
        P(),
        P(),
        P(),
        P(),
    )
    out_specs = P(TABLE_SEQ, None)
    return jax.shard_map(local, mesh=torus, in_specs=in_specs, out_specs=out_specs, check_vma=False)
```

```python
import functools

import jax
import jax.numpy as jnp
from jax import lax
from jax.experimental import pallas as pl
from jax.experimental.pallas import tpu as pltpu
from jax.sharding import Mesh
from jax.sharding import PartitionSpec as P

HEADS = 8
HEAD_DIM = 64
SEQ = ("seq_0", "seq_1")
TABLE_SEQ = ("table", "seq_0", "seq_1")
MESH = pl.DeviceIdType.MESH
CHUNKS = 4
TAKE = 8
PARTS = 2
NT = (((1,), (1,)), ((), ()))


def table_steps(groups):
    chips = groups // 2
    order = [chips // 2]
    for far in range(chips // 2 - 1, 0, -1):
        order += [far, chips - far]
    order.append(0)
    return [(dz, dc) for dz in order for dc in (0, 1)][:-2] + [(0, 1), (0, 0)]


def identity(size_0, size_1, dtype):
    rows = lax.broadcasted_iota(jnp.int32, (size_0, size_1), 0)
    cols = lax.broadcasted_iota(jnp.int32, (size_0, size_1), 1)
    return (rows == cols).astype(dtype)


def swish(half):
    return half + half * jnp.tanh(half)


def normalize(values):
    width = values.shape[-1]
    row_mean = jnp.sum(values, axis=-1, keepdims=True) * (1.0 / width)
    centred = values - row_mean
    variance = jnp.sum(centred * centred, axis=-1, keepdims=True) * (1.0 / width)
    return centred * lax.rsqrt(variance + 1e-06)


def dot(a, b):
    return jnp.dot(a, b, preferred_element_type=jnp.float32)


def dot_nt(a, b):
    return lax.dot_general(a, b, NT, preferred_element_type=jnp.float32)


def build_caches(cache, keys, vals, group_length):
    layers, _, seq_0, part, _ = cache.shape
    hist = seq_0 * part
    pair_dim = 2 * HEAD_DIM
    low = lax.broadcasted_iota(jnp.int32, (hist, pair_dim), 1) < HEAD_DIM
    live = lax.broadcasted_iota(jnp.int32, (hist, pair_dim), 0) < group_length
    zero = jnp.zeros((), jnp.bfloat16)
    for layer in range(layers):
        for p in range(HEADS // 2):
            cols = slice(p * pair_dim, (p + 1) * pair_dim)
            key = cache[layer, 0, :, :, cols].reshape(hist, pair_dim)
            keys[layer, 2 * p] = jnp.where(low, key, zero)
            keys[layer, 2 * p + 1] = jnp.where(low, zero, key)
            val = jnp.where(live, cache[layer, 1, :, :, cols].reshape(hist, pair_dim), zero)
            vals[layer, p, :hist] = jnp.where(low, val, zero)
            vals[layer, p, hist:] = jnp.where(low, zero, val)


def content_block(rows, w_in, w_out, hidden):
    ff = w_in.shape[1]
    step = 512
    half_rows = rows * jnp.bfloat16(0.5)
    for f in range(0, ff, step):
        hidden[:, f : f + step] = swish(dot(half_rows, w_in[:, f : f + step]).astype(jnp.bfloat16))
    return (rows.astype(jnp.float32) + dot(hidden[...], w_out[...])).astype(jnp.bfloat16)


def layers_block(states, w_proj, w_back, keys, vals, weights):
    rows, width = states.shape
    hist = keys.shape[2]
    pair_dim = 2 * HEAD_DIM
    pairs = HEADS // 2
    cut = rows // PARTS
    side = width // 2
    parts = [states[k * cut : (k + 1) * cut] for k in range(PARTS)]
    for layer in range(w_proj.shape[0]):
        queries, gates = [], []
        for part in parts:
            normed = normalize(part.astype(jnp.float32)).astype(jnp.bfloat16) * jnp.bfloat16(0.5)
            queries.append(swish(dot(normed, w_proj[layer, :, width:])).astype(jnp.bfloat16) * jnp.bfloat16(1 / 16))
            gates.append(swish(dot(normed, w_proj[layer, :, :width])))
        query = jnp.concatenate(queries, axis=0)
        attended = [[] for _ in parts]
        for p in range(pairs):
            query_pair = query[:, p * pair_dim : (p + 1) * pair_dim]
            for head in range(2):
                score = dot_nt(query_pair, keys[layer, 2 * p + head])
                weights[p % 2, head] = swish(score.astype(jnp.bfloat16))
            value = [vals[layer, p, head * hist : (head + 1) * hist] for head in range(2)]
            if p < pairs - 1:
                both = dot(weights[p % 2, 0], value[0]) + dot(weights[p % 2, 1], value[1])
                for k in range(PARTS):
                    attended[k].append(both[k * cut : (k + 1) * cut])
            else:
                for k in range(PARTS):
                    own = slice(k * cut, (k + 1) * cut)
                    attended[k].append(dot(weights[p % 2, 0, own], value[0]) + dot(weights[p % 2, 1, own], value[1]))
        after = []
        for part, pieces, gate in zip(parts, attended, gates):
            mixed = (normalize(jnp.concatenate(pieces, axis=1)) * gate).astype(jnp.bfloat16)
            back = [dot(mixed, w_back[layer, :, c : c + side]) for c in range(0, width, side)]
            after.append((part.astype(jnp.float32) + jnp.concatenate(back, axis=1)).astype(jnp.bfloat16))
        parts = after
    return jnp.concatenate(parts, axis=0)


def rank_kernel(
    dims,
    lengths_hbm,
    ids_hbm,
    counts_hbm,
    table_hbm,
    hist_hbm,
    w_in_hbm,
    w_out_hbm,
    w_proj_hbm,
    w_back_hbm,
    out,
    wide,
    lanes_in,
    ids_in,
    ids_low,
    ids,
    counts,
    lengths,
    offsets,
    rows,
    window,
    outgoing,
    emb,
    cache,
    w_in,
    w_out,
    w_proj,
    w_back,
    keys,
    vals,
    hidden,
    weights,
    load_sem,
    weight_sem,
    piece_send,
    piece_recv,
    hist_send,
    hist_recv,
    own_sem,
):
    groups, seq_0, seq_1, vocab, columns, per_sender, cap, hist_rows = dims
    table_index = lax.axis_index("table")
    x = lax.axis_index("seq_0")
    y = lax.axis_index("seq_1")
    shard = x * seq_1 + y
    chips = groups // 2
    z = table_index // 2
    core = table_index % 2
    steps = table_steps(groups)
    x_far = sorted(range(1, seq_0), key=lambda d: -min(d, seq_0 - d))
    y_far = sorted(range(1, seq_1), key=lambda d: -min(d, seq_1 - d))
    senders = groups // CHUNKS
    chunk_rows = senders * per_sender
    chunk_slots = senders * cap

    def table_peer(dz, dc):
        return ((z + dz) % chips) * 2 + (core + dc) % 2

    mine = pl.ds(y * hist_rows, hist_rows)
    load_ids = pltpu.make_async_copy(ids_hbm, ids_in, load_sem.at[0])
    load_table = pltpu.make_async_copy(table_hbm, lanes_in, load_sem.at[1])
    load_counts = pltpu.make_async_copy(counts_hbm.at[:, shard, :], counts, load_sem.at[2])
    load_hist = pltpu.make_async_copy(hist_hbm, cache.at[:, :, x, mine, :], load_sem.at[3])
    load_lengths = pltpu.make_async_copy(lengths_hbm, lengths, load_sem.at[4])
    for load in (load_ids, load_table, load_counts, load_hist, load_lengths):
        load.start()
    sources = (w_in_hbm, w_out_hbm, w_proj_hbm, w_back_hbm)
    targets = (w_in, w_out, w_proj, w_back)
    weight_loads = [pltpu.make_async_copy(s, d, weight_sem.at[i]) for i, (s, d) in enumerate(zip(sources, targets))]

    barrier = pltpu.get_barrier_semaphore()
    for dz, dc in steps[:-1]:
        pl.semaphore_signal(barrier, inc=1, device_id={"table": table_peer(dz, dc)}, device_id_type=MESH)
    for d in x_far:
        pl.semaphore_signal(barrier, inc=1, device_id={"seq_0": (x + d) % seq_0}, device_id_type=MESH)
    for d in y_far:
        pl.semaphore_signal(barrier, inc=1, device_id={"seq_1": (y + d) % seq_1}, device_id_type=MESH)

    load_ids.wait()
    ids_low[...] = ids_in[...] & (vocab - 1)
    move_ids = pltpu.make_async_copy(ids_low, ids, load_sem.at[0])
    move_ids.start()
    load_table.wait()
    for load in weight_loads:
        load.start()
    block = 256
    eye = identity(block, block, jnp.bfloat16)
    blank = jnp.zeros((128 - columns, block), jnp.bfloat16)

    def widen(b, carry):
        at = pl.multiple_of(b * 2 * block, 2 * block)
        piece = jnp.concatenate(
            [lanes_in[:, pl.ds(at, block)], blank, lanes_in[:, pl.ds(at + block, block)], blank], axis=0
        )
        turned = dot_nt(eye, piece)
        wide[pl.ds(at, block), :] = turned[:, :128]
        wide[pl.ds(at + block, block), :] = turned[:, 128:]
        return carry

    lax.fori_loop(0, vocab // (2 * block), widen, 0)

    load_counts.wait()
    load_lengths.wait()

    def offset_row(t, carry):
        total = jnp.int32(0)
        for g in range(groups):
            offsets[t, g] = total
            total = total + counts[t, g]
        return carry

    lax.fori_loop(0, groups, offset_row, 0)
    load_hist.wait()
    pl.semaphore_wait(barrier, len(steps) - 1 + len(x_far) + len(y_far))

    def hist_copy(n, view, axis, to):
        return pltpu.make_async_remote_copy(
            src_ref=view,
            dst_ref=view,
            send_sem=hist_send.at[n],
            recv_sem=hist_recv.at[n],
            device_id={axis: to},
            device_id_type=MESH,
        )

    own_keys = cache.at[:, 0, x, mine, :]
    own_vals = cache.at[:, 1, x, mine, :]
    row_keys = cache.at[:, 0, x, :, :]
    row_vals = cache.at[:, 1, :, mine, :]
    first, second = [], []
    for d in y_far:
        first.append(hist_copy(len(first), own_keys, "seq_1", (y + d) % seq_1))
    for d in x_far:
        first.append(hist_copy(len(first), own_vals, "seq_0", (x + d) % seq_0))
    for d in x_far:
        second.append(hist_copy(len(first) + len(second), row_keys, "seq_0", (x + d) % seq_0))
    for d in y_far:
        second.append(hist_copy(len(first) + len(second), row_vals, "seq_1", (y + d) % seq_1))
    for copy in first:
        copy.start()

    fold = identity(columns, 128, jnp.bfloat16)
    slot_iota = lax.broadcasted_iota(jnp.int32, (cap, 128), 0)

    def own_copy(j):
        here = emb.at[pl.ds(table_index * columns, columns), pl.ds(j * chunk_slots, chunk_slots)]
        return pltpu.make_async_copy(outgoing.at[j, len(steps) - 1], here, own_sem.at[j])

    def piece_copy(j, n):
        dz, dc = steps[n]
        return pltpu.make_async_remote_copy(
            src_ref=outgoing.at[j, n],
            dst_ref=emb.at[pl.ds(table_index * columns, columns), pl.ds(j * chunk_slots, chunk_slots)],
            send_sem=piece_send.at[j, n],
            recv_sem=piece_recv.at[j, n],
            device_id={"table": table_peer(dz, dc)},
            device_id_type=MESH,
        )

    move_ids.wait()
    id_rows = chunk_rows // 128
    places = [table_index // groups + u for u in range(TAKE)]

    def chunk(j, carry):
        def take(i, inner):
            for v in range(128 // TAKE):
                some = ids.at[j * id_rows + i, pl.ds(v * TAKE, TAKE)]
                into = rows.at[pl.ds(pl.multiple_of(i * 128 + v * TAKE, TAKE), TAKE), :]
                for u in range(TAKE):
                    into[u : u + 1, :] = wide[pl.ds(some[places[u]], 1), :]
            return inner

        lax.fori_loop(0, id_rows, take, 0)
        for n, (dz, dc) in enumerate(steps):
            g = table_peer(dz, dc)
            for t in range(senders):
                sender = j * senders + t
                start = offsets[sender, g]
                filled = counts[sender, g]
                taken = rows[pl.ds(start + t * per_sender, cap), :]
                window[n % 2, t * cap : (t + 1) * cap, :] = jnp.where(slot_iota < filled, taken, 0.0).astype(jnp.bfloat16)
            outgoing[j, n] = dot_nt(fold, window[n % 2]).astype(jnp.bfloat16)
            if n < len(steps) - 1:
                piece_copy(j, n).start()
            else:
                own_copy(j).start()

        @pl.when(j == 0)
        def _():
            for copy in first:
                copy.wait()
            for copy in second:
                copy.start()

        return carry

    lax.fori_loop(0, CHUNKS, chunk, 0)

    for load in weight_loads:
        load.wait()
    turn = identity(chunk_slots, chunk_slots, jnp.bfloat16)

    def block_rows(j):
        return pl.ds(pl.multiple_of(j * chunk_slots, chunk_slots), chunk_slots)

    def content(j):
        for n in range(len(steps) - 1):
            piece_copy(j, n).wait()
        own_copy(j).wait()
        content_in = dot_nt(turn, emb[:, block_rows(j)]).astype(jnp.bfloat16)
        out[block_rows(j), :] = content_block(content_in, w_in, w_out, hidden)

    content(0)
    for copy in second:
        copy.wait()
    build_caches(cache, keys, vals, lengths[table_index])

    def run(j, carry):
        @pl.when(j > 0)
        def _():
            content(j)

        out[block_rows(j), :] = layers_block(out[block_rows(j), :], w_proj, w_back, keys, vals, weights)
        return carry

    lax.fori_loop(0, CHUNKS, run, 0)


def local(item_ids, item_table, group_counts, lengths, history, w_in, w_out, w_proj, w_back):
    groups = lax.axis_size("table")
    seq_0, seq_1 = lax.axis_size("seq_0"), lax.axis_size("seq_1")
    vocab, columns = item_table.shape
    per_sender = item_ids.shape[0] // groups
    cap = 3 * per_sender // (2 * groups)
    layers, hist_rows, width = history.shape[1], history.shape[3], history.shape[4]
    hist = hist_rows * seq_0 * seq_1
    slots = groups * cap
    senders = groups // CHUNKS
    block = senders * cap
    dims = (groups, seq_0, seq_1, vocab, columns, per_sender, cap, hist_rows)
    id_rows = item_ids.shape[0] // 128
    in_hbm = pl.BlockSpec(memory_space=pltpu.HBM)
    vmem, dma = pltpu.VMEM, pltpu.SemaphoreType.DMA
    operands = (lengths, item_ids.reshape(id_rows, 128), group_counts, item_table.T, history[0], w_in, w_out, w_proj, w_back)
    operands = [pltpu.with_memory_space_constraint(a, pltpu.HBM) for a in operands]
    return pl.pallas_call(
        functools.partial(rank_kernel, dims),
        out_shape=jax.ShapeDtypeStruct((slots, width), jnp.bfloat16),
        in_specs=[in_hbm] * 9,
        out_specs=pl.BlockSpec(memory_space=pltpu.VMEM),
        scratch_shapes=[
            vmem((vocab, 128), jnp.float32),
            vmem((columns, vocab), jnp.bfloat16),
            vmem((id_rows, 128), jnp.int32),
            vmem((id_rows, 128), jnp.int32),
            pltpu.SMEM((id_rows, 128), jnp.int32),
            pltpu.SMEM((groups, groups), jnp.int32),
            pltpu.SMEM((groups,), jnp.int32),
            pltpu.SMEM((groups, groups), jnp.int32),
            vmem((senders * per_sender + 128, 128), jnp.float32),
            vmem((2, block, 128), jnp.bfloat16),
            vmem((CHUNKS, groups, columns, block), jnp.bfloat16),
            vmem((width, slots), jnp.bfloat16),
            vmem((layers, 2, seq_0, seq_1 * hist_rows, width), jnp.bfloat16),
            vmem(w_in.shape, jnp.bfloat16),
            vmem(w_out.shape, jnp.bfloat16),
            vmem(w_proj.shape, jnp.bfloat16),
            vmem(w_back.shape, jnp.bfloat16),
            vmem((layers, HEADS, hist, 2 * HEAD_DIM), jnp.bfloat16),
            vmem((layers, HEADS // 2, 2 * hist, 2 * HEAD_DIM), jnp.bfloat16),
            vmem((block, w_in.shape[1]), jnp.bfloat16),
            vmem((2, 2, block, hist), jnp.bfloat16),
            dma((5,)),
            dma((4,)),
            dma((CHUNKS, groups)),
            dma((CHUNKS, groups)),
            dma((2 * (seq_0 + seq_1 - 2),)),
            dma((2 * (seq_0 + seq_1 - 2),)),
            dma((CHUNKS,)),
        ],
        compiler_params=pltpu.CompilerParams(
            collective_id=0, has_side_effects=True, vmem_limit_bytes=50 * 1024 * 1024
        ),
        name="rank",
    )(*operands)


def solution(mesh):
    torus = Mesh(mesh.devices.reshape(mesh.shape["table"], 4, 4), ("table", "seq_0", "seq_1"))
    in_specs = (
        P(SEQ),
        P(SEQ, "table"),
        P(),
        P(),
        P("table", None, None, SEQ, None),
        P(),
        P(),
        P(),
        P(),
    )
    out_specs = P(TABLE_SEQ, None)
    return jax.shard_map(local, mesh=torus, in_specs=in_specs, out_specs=out_specs, check_vma=False)
```

```python
import functools

import jax
import jax.numpy as jnp
from jax import lax
from jax.experimental import pallas as pl
from jax.experimental.pallas import tpu as pltpu
from jax.sharding import Mesh
from jax.sharding import PartitionSpec as P

HEADS = 8
HEAD_DIM = 64
SEQ = ("seq_0", "seq_1")
TABLE_SEQ = ("table", "seq_0", "seq_1")
MESH = pl.DeviceIdType.MESH
CHUNKS = 4
TAKE = 8
PARTS = 2
WIDEN = 4
NT = (((1,), (1,)), ((), ()))


def table_steps(groups):
    chips = groups // 2
    order = [chips // 2]
    for far in range(chips // 2 - 1, 0, -1):
        order += [far, chips - far]
    order.append(0)
    return [(dz, dc) for dz in order for dc in (0, 1)][:-2] + [(0, 1), (0, 0)]


def identity(size_0, size_1, dtype):
    rows = lax.broadcasted_iota(jnp.int32, (size_0, size_1), 0)
    cols = lax.broadcasted_iota(jnp.int32, (size_0, size_1), 1)
    return (rows == cols).astype(dtype)


def swish(half):
    return half + half * jnp.tanh(half)


def normalize(values):
    width = values.shape[-1]
    row_mean = jnp.sum(values, axis=-1, keepdims=True) * (1.0 / width)
    centred = values - row_mean
    variance = jnp.sum(centred * centred, axis=-1, keepdims=True) * (1.0 / width)
    return centred * lax.rsqrt(variance + 1e-06)


def dot(a, b):
    return jnp.dot(a, b, preferred_element_type=jnp.float32)


def dot_nt(a, b):
    return lax.dot_general(a, b, NT, preferred_element_type=jnp.float32)


def build_caches(cache, keys, vals, group_length):
    layers, _, seq_0, part, _ = cache.shape
    hist = seq_0 * part
    pair_dim = 2 * HEAD_DIM
    low = lax.broadcasted_iota(jnp.int32, (hist, pair_dim), 1) < HEAD_DIM
    live = lax.broadcasted_iota(jnp.int32, (hist, pair_dim), 0) < group_length
    zero = jnp.zeros((), jnp.bfloat16)
    for layer in range(layers):
        for p in range(HEADS // 2):
            cols = slice(p * pair_dim, (p + 1) * pair_dim)
            key = cache[layer, 0, :, :, cols].reshape(hist, pair_dim)
            keys[layer, 2 * p] = jnp.where(low, key, zero)
            keys[layer, 2 * p + 1] = jnp.where(low, zero, key)
            val = jnp.where(live, cache[layer, 1, :, :, cols].reshape(hist, pair_dim), zero)
            vals[layer, p, :hist] = jnp.where(low, val, zero)
            vals[layer, p, hist:] = jnp.where(low, zero, val)


def content_block(rows, w_in, w_out, hidden):
    ff = w_in.shape[1]
    step = 512
    half_rows = rows * jnp.bfloat16(0.5)
    for f in range(0, ff, step):
        hidden[:, f : f + step] = swish(dot(half_rows, w_in[:, f : f + step]).astype(jnp.bfloat16))
    return (rows.astype(jnp.float32) + dot(hidden[...], w_out[...])).astype(jnp.bfloat16)


def layers_block(states, w_proj, w_back, keys, vals, weights):
    rows, width = states.shape
    hist = keys.shape[2]
    pair_dim = 2 * HEAD_DIM
    pairs = HEADS // 2
    cut = rows // PARTS
    side = width // 2
    parts = [states[k * cut : (k + 1) * cut] for k in range(PARTS)]
    for layer in range(w_proj.shape[0]):
        queries, gates = [], []
        for part in parts:
            normed = normalize(part.astype(jnp.float32)).astype(jnp.bfloat16) * jnp.bfloat16(0.5)
            queries.append(swish(dot(normed, w_proj[layer, :, width:])).astype(jnp.bfloat16) * jnp.bfloat16(1 / 16))
            gates.append(swish(dot(normed, w_proj[layer, :, :width])))
        query = jnp.concatenate(queries, axis=0)
        attended = [[] for _ in parts]
        for p in range(pairs):
            query_pair = query[:, p * pair_dim : (p + 1) * pair_dim]
            for head in range(2):
                score = dot_nt(query_pair, keys[layer, 2 * p + head])
                weights[p % 2, head] = swish(score.astype(jnp.bfloat16))
            value = [vals[layer, p, head * hist : (head + 1) * hist] for head in range(2)]
            if p < pairs - 1:
                both = dot(weights[p % 2, 0], value[0]) + dot(weights[p % 2, 1], value[1])
                for k in range(PARTS):
                    attended[k].append(both[k * cut : (k + 1) * cut])
            else:
                for k in range(PARTS):
                    own = slice(k * cut, (k + 1) * cut)
                    attended[k].append(dot(weights[p % 2, 0, own], value[0]) + dot(weights[p % 2, 1, own], value[1]))
        after = []
        for part, pieces, gate in zip(parts, attended, gates):
            mixed = (normalize(jnp.concatenate(pieces, axis=1)) * gate).astype(jnp.bfloat16)
            back = [dot(mixed, w_back[layer, :, c : c + side]) for c in range(0, width, side)]
            after.append((part.astype(jnp.float32) + jnp.concatenate(back, axis=1)).astype(jnp.bfloat16))
        parts = after
    return jnp.concatenate(parts, axis=0)


def rank_kernel(
    dims,
    lengths_hbm,
    ids_hbm,
    counts_hbm,
    table_hbm,
    hist_hbm,
    w_in_hbm,
    w_out_hbm,
    w_proj_hbm,
    w_back_hbm,
    out,
    wide,
    lanes_in,
    ids_in,
    ids_low,
    ids,
    counts,
    lengths,
    offsets,
    rows,
    window,
    outgoing,
    emb,
    cache,
    w_in,
    w_out,
    w_proj,
    w_back,
    keys,
    vals,
    hidden,
    weights,
    load_sem,
    weight_sem,
    piece_send,
    piece_recv,
    hist_send,
    hist_recv,
    own_sem,
):
    groups, seq_0, seq_1, vocab, columns, per_sender, cap, hist_rows = dims
    table_index = lax.axis_index("table")
    x = lax.axis_index("seq_0")
    y = lax.axis_index("seq_1")
    shard = x * seq_1 + y
    chips = groups // 2
    z = table_index // 2
    core = table_index % 2
    steps = table_steps(groups)
    x_far = sorted(range(1, seq_0), key=lambda d: -min(d, seq_0 - d))
    y_far = sorted(range(1, seq_1), key=lambda d: -min(d, seq_1 - d))
    senders = groups // CHUNKS
    chunk_rows = senders * per_sender
    chunk_slots = senders * cap

    def table_peer(dz, dc):
        return ((z + dz) % chips) * 2 + (core + dc) % 2

    mine = pl.ds(y * hist_rows, hist_rows)
    load_ids = pltpu.make_async_copy(ids_hbm, ids_in, load_sem.at[0])
    load_table = pltpu.make_async_copy(table_hbm, lanes_in, load_sem.at[1])
    load_counts = pltpu.make_async_copy(counts_hbm.at[:, shard, :], counts, load_sem.at[2])
    load_hist = pltpu.make_async_copy(hist_hbm, cache.at[:, :, x, mine, :], load_sem.at[3])
    load_lengths = pltpu.make_async_copy(lengths_hbm, lengths, load_sem.at[4])
    for load in (load_ids, load_table, load_counts, load_hist, load_lengths):
        load.start()
    sources = (w_in_hbm, w_out_hbm, w_proj_hbm, w_back_hbm)
    targets = (w_in, w_out, w_proj, w_back)
    weight_loads = [pltpu.make_async_copy(s, d, weight_sem.at[i]) for i, (s, d) in enumerate(zip(sources, targets))]

    barrier = pltpu.get_barrier_semaphore()
    for dz, dc in steps[:-1]:
        pl.semaphore_signal(barrier, inc=1, device_id={"table": table_peer(dz, dc)}, device_id_type=MESH)
    for d in x_far:
        pl.semaphore_signal(barrier, inc=1, device_id={"seq_0": (x + d) % seq_0}, device_id_type=MESH)
    for d in y_far:
        pl.semaphore_signal(barrier, inc=1, device_id={"seq_1": (y + d) % seq_1}, device_id_type=MESH)

    load_ids.wait()
    ids_low[...] = ids_in[...] & (vocab - 1)
    move_ids = pltpu.make_async_copy(ids_low, ids, load_sem.at[0])
    move_ids.start()
    load_table.wait()
    for load in weight_loads:
        load.start()
    block = 256
    eye = identity(block, block, jnp.bfloat16)
    blank = jnp.zeros((128 - columns, block), jnp.bfloat16)

    def widen(b, carry):
        for k in range(WIDEN):
            at = pl.multiple_of((b * WIDEN + k) * 2 * block, 2 * block)
            piece = jnp.concatenate(
                [lanes_in[:, pl.ds(at, block)], blank, lanes_in[:, pl.ds(at + block, block)], blank], axis=0
            )
            turned = dot_nt(eye, piece)
            wide[pl.ds(at, block), :] = turned[:, :128]
            wide[pl.ds(at + block, block), :] = turned[:, 128:]
        return carry

    lax.fori_loop(0, vocab // (2 * block * WIDEN), widen, 0)

    load_counts.wait()
    load_lengths.wait()

    def offset_row(t, carry):
        total = jnp.int32(0)
        for g in range(groups):
            offsets[t, g] = total
            total = total + counts[t, g]
        return carry

    lax.fori_loop(0, groups, offset_row, 0)
    load_hist.wait()
    pl.semaphore_wait(barrier, len(steps) - 1 + len(x_far) + len(y_far))

    def hist_copy(n, view, axis, to):
        return pltpu.make_async_remote_copy(
            src_ref=view,
            dst_ref=view,
            send_sem=hist_send.at[n],
            recv_sem=hist_recv.at[n],
            device_id={axis: to},
            device_id_type=MESH,
        )

    own_keys = cache.at[:, 0, x, mine, :]
    own_vals = cache.at[:, 1, x, mine, :]
    row_keys = cache.at[:, 0, x, :, :]
    row_vals = cache.at[:, 1, :, mine, :]
    first, second = [], []
    for d in y_far:
        first.append(hist_copy(len(first), own_keys, "seq_1", (y + d) % seq_1))
    for d in x_far:
        first.append(hist_copy(len(first), own_vals, "seq_0", (x + d) % seq_0))
    for d in x_far:
        second.append(hist_copy(len(first) + len(second), row_keys, "seq_0", (x + d) % seq_0))
    for d in y_far:
        second.append(hist_copy(len(first) + len(second), row_vals, "seq_1", (y + d) % seq_1))
    for copy in first:
        copy.start()

    fold = identity(columns, 128, jnp.bfloat16)
    slot_iota = lax.broadcasted_iota(jnp.int32, (cap, 128), 0)

    def own_copy(j):
        here = emb.at[pl.ds(table_index * columns, columns), pl.ds(j * chunk_slots, chunk_slots)]
        return pltpu.make_async_copy(outgoing.at[j, len(steps) - 1], here, own_sem.at[j])

    def piece_copy(j, n):
        dz, dc = steps[n]
        return pltpu.make_async_remote_copy(
            src_ref=outgoing.at[j, n],
            dst_ref=emb.at[pl.ds(table_index * columns, columns), pl.ds(j * chunk_slots, chunk_slots)],
            send_sem=piece_send.at[j, n],
            recv_sem=piece_recv.at[j, n],
            device_id={"table": table_peer(dz, dc)},
            device_id_type=MESH,
        )

    move_ids.wait()
    id_rows = chunk_rows // 128
    places = [table_index // groups + u for u in range(TAKE)]

    def send(j):
        for n in range(len(steps) - 1):
            piece_copy(j, n).start()
        own_copy(j).start()

    def chunk(j, carry):
        def take(i, inner):
            for v in range(128 // TAKE):
                some = ids.at[j * id_rows + i, pl.ds(v * TAKE, TAKE)]
                into = rows.at[pl.ds(pl.multiple_of(i * 128 + v * TAKE, TAKE), TAKE), :]
                for u in range(TAKE):
                    into[u : u + 1, :] = wide[pl.ds(some[places[u]], 1), :]
            return inner

        lax.fori_loop(0, id_rows, take, 0)

        @pl.when(j == 1)
        def _():
            for copy in first:
                copy.wait()
            for copy in second:
                copy.start()

        for n, (dz, dc) in enumerate(steps):
            g = table_peer(dz, dc)
            for t in range(senders):
                sender = j * senders + t
                start = offsets[sender, g]
                filled = counts[sender, g]
                taken = rows[pl.ds(start + t * per_sender, cap), :]
                window[n % 2, t * cap : (t + 1) * cap, :] = jnp.where(slot_iota < filled, taken, 0.0).astype(jnp.bfloat16)
            outgoing[j, n] = dot_nt(fold, window[n % 2]).astype(jnp.bfloat16)

        @pl.when(j == 0)
        def _():
            send(j)

        @pl.when(j > 1)
        def _():
            send(j - 1)

        return carry

    lax.fori_loop(0, CHUNKS, chunk, 0)

    for load in weight_loads:
        load.wait()
    turn = identity(chunk_slots, chunk_slots, jnp.bfloat16)

    def block_rows(j):
        return pl.ds(pl.multiple_of(j * chunk_slots, chunk_slots), chunk_slots)

    def content(j):
        for n in range(len(steps) - 1):
            piece_copy(j, n).wait()
        own_copy(j).wait()
        content_in = dot_nt(turn, emb[:, block_rows(j)]).astype(jnp.bfloat16)
        out[block_rows(j), :] = content_block(content_in, w_in, w_out, hidden)

    content(0)
    send(CHUNKS - 1)
    for copy in second:
        copy.wait()
    build_caches(cache, keys, vals, lengths[table_index])

    def run(j, carry):
        @pl.when(j > 0)
        def _():
            content(j)

        out[block_rows(j), :] = layers_block(out[block_rows(j), :], w_proj, w_back, keys, vals, weights)
        return carry

    lax.fori_loop(0, CHUNKS, run, 0)


def local(item_ids, item_table, group_counts, lengths, history, w_in, w_out, w_proj, w_back):
    groups = lax.axis_size("table")
    seq_0, seq_1 = lax.axis_size("seq_0"), lax.axis_size("seq_1")
    vocab, columns = item_table.shape
    per_sender = item_ids.shape[0] // groups
    cap = 3 * per_sender // (2 * groups)
    layers, hist_rows, width = history.shape[1], history.shape[3], history.shape[4]
    hist = hist_rows * seq_0 * seq_1
    slots = groups * cap
    senders = groups // CHUNKS
    block = senders * cap
    dims = (groups, seq_0, seq_1, vocab, columns, per_sender, cap, hist_rows)
    id_rows = item_ids.shape[0] // 128
    in_hbm = pl.BlockSpec(memory_space=pltpu.HBM)
    vmem, dma = pltpu.VMEM, pltpu.SemaphoreType.DMA
    operands = (lengths, item_ids.reshape(id_rows, 128), group_counts, item_table.T, history[0], w_in, w_out, w_proj, w_back)
    operands = [pltpu.with_memory_space_constraint(a, pltpu.HBM) for a in operands]
    return pl.pallas_call(
        functools.partial(rank_kernel, dims),
        out_shape=jax.ShapeDtypeStruct((slots, width), jnp.bfloat16),
        in_specs=[in_hbm] * 9,
        out_specs=pl.BlockSpec(memory_space=pltpu.VMEM),
        scratch_shapes=[
            vmem((vocab, 128), jnp.float32),
            vmem((columns, vocab), jnp.bfloat16),
            vmem((id_rows, 128), jnp.int32),
            vmem((id_rows, 128), jnp.int32),
            pltpu.SMEM((id_rows, 128), jnp.int32),
            pltpu.SMEM((groups, groups), jnp.int32),
            pltpu.SMEM((groups,), jnp.int32),
            pltpu.SMEM((groups, groups), jnp.int32),
            vmem((senders * per_sender + 128, 128), jnp.float32),
            vmem((2, block, 128), jnp.bfloat16),
            vmem((CHUNKS, groups, columns, block), jnp.bfloat16),
            vmem((width, slots), jnp.bfloat16),
            vmem((layers, 2, seq_0, seq_1 * hist_rows, width), jnp.bfloat16),
            vmem(w_in.shape, jnp.bfloat16),
            vmem(w_out.shape, jnp.bfloat16),
            vmem(w_proj.shape, jnp.bfloat16),
            vmem(w_back.shape, jnp.bfloat16),
            vmem((layers, HEADS, hist, 2 * HEAD_DIM), jnp.bfloat16),
            vmem((layers, HEADS // 2, 2 * hist, 2 * HEAD_DIM), jnp.bfloat16),
            vmem((block, w_in.shape[1]), jnp.bfloat16),
            vmem((2, 2, block, hist), jnp.bfloat16),
            dma((5,)),
            dma((4,)),
            dma((CHUNKS, groups)),
            dma((CHUNKS, groups)),
            dma((2 * (seq_0 + seq_1 - 2),)),
            dma((2 * (seq_0 + seq_1 - 2),)),
            dma((CHUNKS,)),
        ],
        compiler_params=pltpu.CompilerParams(
            collective_id=0, has_side_effects=True, vmem_limit_bytes=50 * 1024 * 1024
        ),
        name="rank",
    )(*operands)


def solution(mesh):
    torus = Mesh(mesh.devices.reshape(mesh.shape["table"], 4, 4), ("table", "seq_0", "seq_1"))
    in_specs = (
        P(SEQ),
        P(SEQ, "table"),
        P(),
        P(),
        P("table", None, None, SEQ, None),
        P(),
        P(),
        P(),
        P(),
    )
    out_specs = P(TABLE_SEQ, None)
    return jax.shard_map(local, mesh=torus, in_specs=in_specs, out_specs=out_specs, check_vma=False)
```

```python
import functools

import jax
import jax.numpy as jnp
from jax import lax
from jax.experimental import pallas as pl
from jax.experimental.pallas import tpu as pltpu
from jax.sharding import Mesh
from jax.sharding import PartitionSpec as P

HEADS = 8
HEAD_DIM = 64
SEQ = ("seq_0", "seq_1")
TABLE_SEQ = ("table", "seq_0", "seq_1")
MESH = pl.DeviceIdType.MESH
CHUNKS = 4
TAKE = 8
PARTS = 2
WIDEN = 16
NT = (((1,), (1,)), ((), ()))


def table_steps(groups):
    chips = groups // 2
    order = [chips // 2]
    for far in range(chips // 2 - 1, 0, -1):
        order += [far, chips - far]
    order.append(0)
    return [(dz, dc) for dz in order for dc in (0, 1)][:-2] + [(0, 1), (0, 0)]


def identity(size_0, size_1, dtype):
    rows = lax.broadcasted_iota(jnp.int32, (size_0, size_1), 0)
    cols = lax.broadcasted_iota(jnp.int32, (size_0, size_1), 1)
    return (rows == cols).astype(dtype)


def swish(half):
    return half + half * jnp.tanh(half)


def normalize(values):
    width = values.shape[-1]
    row_mean = jnp.sum(values, axis=-1, keepdims=True) * (1.0 / width)
    centred = values - row_mean
    variance = jnp.sum(centred * centred, axis=-1, keepdims=True) * (1.0 / width)
    return centred * lax.rsqrt(variance + 1e-06)


def dot(a, b):
    return jnp.dot(a, b, preferred_element_type=jnp.float32)


def dot_nt(a, b):
    return lax.dot_general(a, b, NT, preferred_element_type=jnp.float32)


def build_caches(cache, keys, vals, group_length):
    layers, _, seq_0, part, _ = cache.shape
    hist = seq_0 * part
    pair_dim = 2 * HEAD_DIM
    low = lax.broadcasted_iota(jnp.int32, (hist, pair_dim), 1) < HEAD_DIM
    live = lax.broadcasted_iota(jnp.int32, (hist, pair_dim), 0) < group_length
    zero = jnp.zeros((), jnp.bfloat16)
    for layer in range(layers):
        for p in range(HEADS // 2):
            cols = slice(p * pair_dim, (p + 1) * pair_dim)
            key = cache[layer, 0, :, :, cols].reshape(hist, pair_dim)
            keys[layer, 2 * p] = jnp.where(low, key, zero)
            keys[layer, 2 * p + 1] = jnp.where(low, zero, key)
            val = jnp.where(live, cache[layer, 1, :, :, cols].reshape(hist, pair_dim), zero)
            vals[layer, p, :hist] = jnp.where(low, val, zero)
            vals[layer, p, hist:] = jnp.where(low, zero, val)


def content_block(rows, w_in, w_out, hidden):
    ff = w_in.shape[1]
    step = 512
    half_rows = rows * jnp.bfloat16(0.5)
    for f in range(0, ff, step):
        hidden[:, f : f + step] = swish(dot(half_rows, w_in[:, f : f + step]).astype(jnp.bfloat16))
    return (rows.astype(jnp.float32) + dot(hidden[...], w_out[...])).astype(jnp.bfloat16)


def layers_block(states, w_proj, w_back, keys, vals, weights):
    rows, width = states.shape
    hist = keys.shape[2]
    pair_dim = 2 * HEAD_DIM
    pairs = HEADS // 2
    cut = rows // PARTS
    side = width // 2
    parts = [states[k * cut : (k + 1) * cut] for k in range(PARTS)]
    for layer in range(w_proj.shape[0]):
        queries, gates = [], []
        for part in parts:
            normed = normalize(part.astype(jnp.float32)).astype(jnp.bfloat16) * jnp.bfloat16(0.5)
            queries.append(swish(dot(normed, w_proj[layer, :, width:])).astype(jnp.bfloat16) * jnp.bfloat16(1 / 16))
            gates.append(swish(dot(normed, w_proj[layer, :, :width])))
        query = jnp.concatenate(queries, axis=0)
        attended = [[] for _ in parts]
        for p in range(pairs):
            query_pair = query[:, p * pair_dim : (p + 1) * pair_dim]
            for head in range(2):
                score = dot_nt(query_pair, keys[layer, 2 * p + head])
                weights[p % 2, head] = swish(score.astype(jnp.bfloat16))
            value = [vals[layer, p, head * hist : (head + 1) * hist] for head in range(2)]
            if p < pairs - 1:
                both = dot(weights[p % 2, 0], value[0]) + dot(weights[p % 2, 1], value[1])
                for k in range(PARTS):
                    attended[k].append(both[k * cut : (k + 1) * cut])
            else:
                for k in range(PARTS):
                    own = slice(k * cut, (k + 1) * cut)
                    attended[k].append(dot(weights[p % 2, 0, own], value[0]) + dot(weights[p % 2, 1, own], value[1]))
        after = []
        for part, pieces, gate in zip(parts, attended, gates):
            mixed = (normalize(jnp.concatenate(pieces, axis=1)) * gate).astype(jnp.bfloat16)
            back = [dot(mixed, w_back[layer, :, c : c + side]) for c in range(0, width, side)]
            after.append((part.astype(jnp.float32) + jnp.concatenate(back, axis=1)).astype(jnp.bfloat16))
        parts = after
    return jnp.concatenate(parts, axis=0)


def rank_kernel(
    dims,
    lengths_hbm,
    ids_hbm,
    counts_hbm,
    table_hbm,
    hist_hbm,
    w_in_hbm,
    w_out_hbm,
    w_proj_hbm,
    w_back_hbm,
    out,
    wide,
    lanes_in,
    ids_in,
    ids_low,
    ids,
    counts,
    lengths,
    offsets,
    rows,
    window,
    outgoing,
    emb,
    cache,
    w_in,
    w_out,
    w_proj,
    w_back,
    keys,
    vals,
    hidden,
    weights,
    load_sem,
    table_sem,
    weight_sem,
    piece_send,
    piece_recv,
    hist_send,
    hist_recv,
    own_sem,
):
    groups, seq_0, seq_1, vocab, columns, per_sender, cap, hist_rows = dims
    table_index = lax.axis_index("table")
    x = lax.axis_index("seq_0")
    y = lax.axis_index("seq_1")
    shard = x * seq_1 + y
    chips = groups // 2
    z = table_index // 2
    core = table_index % 2
    steps = table_steps(groups)
    x_far = sorted(range(1, seq_0), key=lambda d: -min(d, seq_0 - d))
    y_far = sorted(range(1, seq_1), key=lambda d: -min(d, seq_1 - d))
    senders = groups // CHUNKS
    chunk_rows = senders * per_sender
    chunk_slots = senders * cap

    def table_peer(dz, dc):
        return ((z + dz) % chips) * 2 + (core + dc) % 2

    mine = pl.ds(y * hist_rows, hist_rows)
    load_ids = pltpu.make_async_copy(ids_hbm, ids_in, load_sem.at[0])
    table_part = 512 * WIDEN
    table_loads = vocab // table_part

    def table_load(c):
        part = pl.ds(pl.multiple_of(c * table_part, table_part), table_part)
        return pltpu.make_async_copy(table_hbm.at[:, part], lanes_in.at[:, part], table_sem.at[c])

    load_counts = pltpu.make_async_copy(counts_hbm.at[:, shard, :], counts, load_sem.at[2])
    load_hist = pltpu.make_async_copy(hist_hbm, cache.at[:, :, x, mine, :], load_sem.at[3])
    load_lengths = pltpu.make_async_copy(lengths_hbm, lengths, load_sem.at[4])
    for load in (load_ids, load_counts, load_lengths, *map(table_load, range(table_loads)), load_hist):
        load.start()
    sources = (w_in_hbm, w_out_hbm, w_proj_hbm, w_back_hbm)
    targets = (w_in, w_out, w_proj, w_back)
    weight_loads = [pltpu.make_async_copy(s, d, weight_sem.at[i]) for i, (s, d) in enumerate(zip(sources, targets))]

    barrier = pltpu.get_barrier_semaphore()
    for dz, dc in steps[:-1]:
        pl.semaphore_signal(barrier, inc=1, device_id={"table": table_peer(dz, dc)}, device_id_type=MESH)
    for d in x_far:
        pl.semaphore_signal(barrier, inc=1, device_id={"seq_0": (x + d) % seq_0}, device_id_type=MESH)
    for d in y_far:
        pl.semaphore_signal(barrier, inc=1, device_id={"seq_1": (y + d) % seq_1}, device_id_type=MESH)

    load_ids.wait()
    ids_low[...] = ids_in[...] & (vocab - 1)
    move_ids = pltpu.make_async_copy(ids_low, ids, load_sem.at[0])
    move_ids.start()
    load_counts.wait()
    load_lengths.wait()

    def offset_row(t, carry):
        total = jnp.int32(0)
        for g in range(groups):
            offsets[t, g] = total
            total = total + counts[t, g]
        return carry

    lax.fori_loop(0, groups, offset_row, 0)
    block = 256
    eye = identity(block, block, jnp.bfloat16)
    blank = jnp.zeros((128 - columns, block), jnp.bfloat16)

    def widen(b, carry):
        table_load(b).wait()
        for k in range(WIDEN):
            at = pl.multiple_of((b * WIDEN + k) * 2 * block, 2 * block)
            piece = jnp.concatenate(
                [lanes_in[:, pl.ds(at, block)], blank, lanes_in[:, pl.ds(at + block, block)], blank], axis=0
            )
            turned = dot_nt(eye, piece)
            wide[pl.ds(at, block), :] = turned[:, :128]
            wide[pl.ds(at + block, block), :] = turned[:, 128:]
        return carry

    lax.fori_loop(0, table_loads, widen, 0)
    for load in weight_loads:
        load.start()

    load_hist.wait()
    pl.semaphore_wait(barrier, len(steps) - 1 + len(x_far) + len(y_far))

    def hist_copy(n, view, axis, to):
        return pltpu.make_async_remote_copy(
            src_ref=view,
            dst_ref=view,
            send_sem=hist_send.at[n],
            recv_sem=hist_recv.at[n],
            device_id={axis: to},
            device_id_type=MESH,
        )

    own_keys = cache.at[:, 0, x, mine, :]
    own_vals = cache.at[:, 1, x, mine, :]
    row_keys = cache.at[:, 0, x, :, :]
    row_vals = cache.at[:, 1, :, mine, :]
    first, second = [], []
    for d in y_far:
        first.append(hist_copy(len(first), own_keys, "seq_1", (y + d) % seq_1))
    for d in x_far:
        first.append(hist_copy(len(first), own_vals, "seq_0", (x + d) % seq_0))
    for d in x_far:
        second.append(hist_copy(len(first) + len(second), row_keys, "seq_0", (x + d) % seq_0))
    for d in y_far:
        second.append(hist_copy(len(first) + len(second), row_vals, "seq_1", (y + d) % seq_1))
    for copy in first:
        copy.start()

    fold = identity(columns, 128, jnp.bfloat16)
    slot_iota = lax.broadcasted_iota(jnp.int32, (cap, 128), 0)

    def own_copy(j):
        here = emb.at[pl.ds(table_index * columns, columns), pl.ds(j * chunk_slots, chunk_slots)]
        return pltpu.make_async_copy(outgoing.at[j, len(steps) - 1], here, own_sem.at[j])

    def piece_copy(j, n):
        dz, dc = steps[n]
        return pltpu.make_async_remote_copy(
            src_ref=outgoing.at[j, n],
            dst_ref=emb.at[pl.ds(table_index * columns, columns), pl.ds(j * chunk_slots, chunk_slots)],
            send_sem=piece_send.at[j, n],
            recv_sem=piece_recv.at[j, n],
            device_id={"table": table_peer(dz, dc)},
            device_id_type=MESH,
        )

    move_ids.wait()
    id_rows = chunk_rows // 128
    places = [table_index // groups + u for u in range(TAKE)]

    def send(j):
        for n in range(len(steps) - 1):
            piece_copy(j, n).start()
        own_copy(j).start()

    def chunk(j, carry):
        def take(i, inner):
            for v in range(128 // TAKE):
                some = ids.at[j * id_rows + i, pl.ds(v * TAKE, TAKE)]
                into = rows.at[pl.ds(pl.multiple_of(i * 128 + v * TAKE, TAKE), TAKE), :]
                for u in range(TAKE):
                    into[u : u + 1, :] = wide[pl.ds(some[places[u]], 1), :]
            return inner

        lax.fori_loop(0, id_rows, take, 0)

        @pl.when(j == 1)
        def _():
            for copy in first:
                copy.wait()
            for copy in second:
                copy.start()

        for n, (dz, dc) in enumerate(steps):
            g = table_peer(dz, dc)
            for t in range(senders):
                sender = j * senders + t
                start = offsets[sender, g]
                filled = counts[sender, g]
                taken = rows[pl.ds(start + t * per_sender, cap), :]
                window[n % 2, t * cap : (t + 1) * cap, :] = jnp.where(slot_iota < filled, taken, 0.0).astype(jnp.bfloat16)
            outgoing[j, n] = dot_nt(fold, window[n % 2]).astype(jnp.bfloat16)

        @pl.when(j == 0)
        def _():
            send(j)

        @pl.when(j > 1)
        def _():
            send(j - 1)

        return carry

    lax.fori_loop(0, CHUNKS, chunk, 0)

    for load in weight_loads:
        load.wait()
    turn = identity(chunk_slots, chunk_slots, jnp.bfloat16)

    def block_rows(j):
        return pl.ds(pl.multiple_of(j * chunk_slots, chunk_slots), chunk_slots)

    def content(j):
        for n in range(len(steps) - 1):
            piece_copy(j, n).wait()
        own_copy(j).wait()
        content_in = dot_nt(turn, emb[:, block_rows(j)]).astype(jnp.bfloat16)
        out[block_rows(j), :] = content_block(content_in, w_in, w_out, hidden)

    content(0)
    send(CHUNKS - 1)
    for copy in second:
        copy.wait()
    build_caches(cache, keys, vals, lengths[table_index])

    def run(j, carry):
        @pl.when(j > 0)
        def _():
            content(j)

        out[block_rows(j), :] = layers_block(out[block_rows(j), :], w_proj, w_back, keys, vals, weights)
        return carry

    lax.fori_loop(0, CHUNKS, run, 0)


def local(item_ids, item_table, group_counts, lengths, history, w_in, w_out, w_proj, w_back):
    groups = lax.axis_size("table")
    seq_0, seq_1 = lax.axis_size("seq_0"), lax.axis_size("seq_1")
    vocab, columns = item_table.shape
    per_sender = item_ids.shape[0] // groups
    cap = 3 * per_sender // (2 * groups)
    layers, hist_rows, width = history.shape[1], history.shape[3], history.shape[4]
    hist = hist_rows * seq_0 * seq_1
    slots = groups * cap
    senders = groups // CHUNKS
    block = senders * cap
    dims = (groups, seq_0, seq_1, vocab, columns, per_sender, cap, hist_rows)
    id_rows = item_ids.shape[0] // 128
    in_hbm = pl.BlockSpec(memory_space=pltpu.HBM)
    vmem, dma = pltpu.VMEM, pltpu.SemaphoreType.DMA
    operands = (lengths, item_ids.reshape(id_rows, 128), group_counts, item_table.T, history[0], w_in, w_out, w_proj, w_back)
    operands = [pltpu.with_memory_space_constraint(a, pltpu.HBM) for a in operands]
    return pl.pallas_call(
        functools.partial(rank_kernel, dims),
        out_shape=jax.ShapeDtypeStruct((slots, width), jnp.bfloat16),
        in_specs=[in_hbm] * 9,
        out_specs=pl.BlockSpec(memory_space=pltpu.VMEM),
        scratch_shapes=[
            vmem((vocab, 128), jnp.float32),
            vmem((columns, vocab), jnp.bfloat16),
            vmem((id_rows, 128), jnp.int32),
            vmem((id_rows, 128), jnp.int32),
            pltpu.SMEM((id_rows, 128), jnp.int32),
            pltpu.SMEM((groups, groups), jnp.int32),
            pltpu.SMEM((groups,), jnp.int32),
            pltpu.SMEM((groups, groups), jnp.int32),
            vmem((senders * per_sender + 128, 128), jnp.float32),
            vmem((2, block, 128), jnp.bfloat16),
            vmem((CHUNKS, groups, columns, block), jnp.bfloat16),
            vmem((width, slots), jnp.bfloat16),
            vmem((layers, 2, seq_0, seq_1 * hist_rows, width), jnp.bfloat16),
            vmem(w_in.shape, jnp.bfloat16),
            vmem(w_out.shape, jnp.bfloat16),
            vmem(w_proj.shape, jnp.bfloat16),
            vmem(w_back.shape, jnp.bfloat16),
            vmem((layers, HEADS, hist, 2 * HEAD_DIM), jnp.bfloat16),
            vmem((layers, HEADS // 2, 2 * hist, 2 * HEAD_DIM), jnp.bfloat16),
            vmem((block, w_in.shape[1]), jnp.bfloat16),
            vmem((2, 2, block, hist), jnp.bfloat16),
            dma((5,)),
            dma((vocab // (512 * WIDEN),)),
            dma((4,)),
            dma((CHUNKS, groups)),
            dma((CHUNKS, groups)),
            dma((2 * (seq_0 + seq_1 - 2),)),
            dma((2 * (seq_0 + seq_1 - 2),)),
            dma((CHUNKS,)),
        ],
        compiler_params=pltpu.CompilerParams(
            collective_id=0, has_side_effects=True, vmem_limit_bytes=50 * 1024 * 1024
        ),
        name="rank",
    )(*operands)


def solution(mesh):
    torus = Mesh(mesh.devices.reshape(mesh.shape["table"], 4, 4), ("table", "seq_0", "seq_1"))
    in_specs = (
        P(SEQ),
        P(SEQ, "table"),
        P(),
        P(),
        P("table", None, None, SEQ, None),
        P(),
        P(),
        P(),
        P(),
    )
    out_specs = P(TABLE_SEQ, None)
    return jax.shard_map(local, mesh=torus, in_specs=in_specs, out_specs=out_specs, check_vma=False)
```

```python
import functools

import jax
import jax.numpy as jnp
from jax import lax
from jax.experimental import pallas as pl
from jax.experimental.pallas import tpu as pltpu
from jax.sharding import Mesh
from jax.sharding import PartitionSpec as P

HEADS = 8
HEAD_DIM = 64
SEQ = ("seq_0", "seq_1")
TABLE_SEQ = ("table", "seq_0", "seq_1")
MESH = pl.DeviceIdType.MESH
CHUNKS = 4
TAKE = 8
PARTS = 2
WIDEN = 16
NT = (((1,), (1,)), ((), ()))


def table_steps(groups):
    chips = groups // 2
    order = [chips // 2]
    for far in range(chips // 2 - 1, 0, -1):
        order += [far, chips - far]
    order.append(0)
    return [(dz, dc) for dz in order for dc in (0, 1)][:-2] + [(0, 1), (0, 0)]


def identity(size_0, size_1, dtype):
    rows = lax.broadcasted_iota(jnp.int32, (size_0, size_1), 0)
    cols = lax.broadcasted_iota(jnp.int32, (size_0, size_1), 1)
    return (rows == cols).astype(dtype)


def swish(half):
    return half + half * jnp.tanh(half)


def normalize(values):
    width = values.shape[-1]
    row_mean = jnp.sum(values, axis=-1, keepdims=True) * (1.0 / width)
    centred = values - row_mean
    variance = jnp.sum(centred * centred, axis=-1, keepdims=True) * (1.0 / width)
    return centred * lax.rsqrt(variance + 1e-06)


def dot(a, b):
    return jnp.dot(a, b, preferred_element_type=jnp.float32)


def dot_nt(a, b):
    return lax.dot_general(a, b, NT, preferred_element_type=jnp.float32)


def build_caches(cache, keys, vals, group_length):
    layers, _, seq_0, part, _ = cache.shape
    hist = seq_0 * part
    pair_dim = 2 * HEAD_DIM
    low = lax.broadcasted_iota(jnp.int32, (hist, pair_dim), 1) < HEAD_DIM
    live = lax.broadcasted_iota(jnp.int32, (hist, pair_dim), 0) < group_length
    zero = jnp.zeros((), jnp.bfloat16)
    for layer in range(layers):
        for p in range(HEADS // 2):
            cols = slice(p * pair_dim, (p + 1) * pair_dim)
            key = cache[layer, 0, :, :, cols].reshape(hist, pair_dim)
            keys[layer, 2 * p] = jnp.where(low, key, zero)
            keys[layer, 2 * p + 1] = jnp.where(low, zero, key)
            val = jnp.where(live, cache[layer, 1, :, :, cols].reshape(hist, pair_dim), zero)
            vals[layer, p, :hist] = jnp.where(low, val, zero)
            vals[layer, p, hist:] = jnp.where(low, zero, val)


def content_block(rows, w_in, w_out, hidden):
    ff = w_in.shape[1]
    step = 512
    half_rows = rows * jnp.bfloat16(0.5)
    for f in range(0, ff, step):
        hidden[:, f : f + step] = swish(dot(half_rows, w_in[:, f : f + step]).astype(jnp.bfloat16))
    return (rows.astype(jnp.float32) + dot(hidden[...], w_out[...])).astype(jnp.bfloat16)


def layers_block(states, w_proj, w_back, keys, vals, weights):
    rows, width = states.shape
    hist = keys.shape[2]
    pair_dim = 2 * HEAD_DIM
    pairs = HEADS // 2
    cut = rows // PARTS
    side = width // 2
    parts = [states[k * cut : (k + 1) * cut] for k in range(PARTS)]
    for layer in range(w_proj.shape[0]):
        queries, gates = [], []
        for part in parts:
            normed = normalize(part.astype(jnp.float32)).astype(jnp.bfloat16) * jnp.bfloat16(0.5)
            queries.append(swish(dot(normed, w_proj[layer, :, width:])).astype(jnp.bfloat16) * jnp.bfloat16(1 / 16))
            gates.append(swish(dot(normed, w_proj[layer, :, :width])))
        query = jnp.concatenate(queries, axis=0)
        attended = [[] for _ in parts]
        for p in range(pairs):
            query_pair = query[:, p * pair_dim : (p + 1) * pair_dim]
            for head in range(2):
                score = dot_nt(query_pair, keys[layer, 2 * p + head])
                weights[p % 2, head] = swish(score.astype(jnp.bfloat16))
            value = [vals[layer, p, head * hist : (head + 1) * hist] for head in range(2)]
            if p < pairs - 1:
                both = dot(weights[p % 2, 0], value[0]) + dot(weights[p % 2, 1], value[1])
                for k in range(PARTS):
                    attended[k].append(both[k * cut : (k + 1) * cut])
            else:
                for k in range(PARTS):
                    own = slice(k * cut, (k + 1) * cut)
                    attended[k].append(dot(weights[p % 2, 0, own], value[0]) + dot(weights[p % 2, 1, own], value[1]))
        after = []
        for part, pieces, gate in zip(parts, attended, gates):
            mixed = (normalize(jnp.concatenate(pieces, axis=1)) * gate).astype(jnp.bfloat16)
            back = [dot(mixed, w_back[layer, :, c : c + side]) for c in range(0, width, side)]
            after.append((part.astype(jnp.float32) + jnp.concatenate(back, axis=1)).astype(jnp.bfloat16))
        parts = after
    return jnp.concatenate(parts, axis=0)


def rank_kernel(
    dims,
    lengths_hbm,
    ids_hbm,
    counts_hbm,
    table_hbm,
    hist_hbm,
    w_in_hbm,
    w_out_hbm,
    w_proj_hbm,
    w_back_hbm,
    out,
    wide,
    lanes_in,
    ids_in,
    ids_low,
    ids,
    counts,
    lengths,
    offsets,
    rows,
    window,
    outgoing,
    emb,
    cache,
    w_in,
    w_out,
    w_proj,
    w_back,
    keys,
    vals,
    hidden,
    weights,
    load_sem,
    table_sem,
    weight_sem,
    piece_send,
    piece_recv,
    hist_send,
    hist_recv,
    own_sem,
):
    groups, seq_0, seq_1, vocab, columns, per_sender, cap, hist_rows = dims
    table_index = lax.axis_index("table")
    x = lax.axis_index("seq_0")
    y = lax.axis_index("seq_1")
    shard = x * seq_1 + y
    chips = groups // 2
    z = table_index // 2
    core = table_index % 2
    steps = table_steps(groups)
    x_far = sorted(range(1, seq_0), key=lambda d: -min(d, seq_0 - d))
    y_far = sorted(range(1, seq_1), key=lambda d: -min(d, seq_1 - d))
    senders = groups // CHUNKS
    chunk_rows = senders * per_sender
    chunk_slots = senders * cap

    def table_peer(dz, dc):
        return ((z + dz) % chips) * 2 + (core + dc) % 2

    mine = pl.ds(y * hist_rows, hist_rows)
    load_ids = pltpu.make_async_copy(ids_hbm, ids_in, load_sem.at[0])
    table_part = 512 * WIDEN
    table_loads = vocab // table_part

    def table_load(c):
        part = pl.ds(pl.multiple_of(c * table_part, table_part), table_part)
        return pltpu.make_async_copy(table_hbm.at[:, part], lanes_in.at[:, part], table_sem.at[c])

    load_counts = pltpu.make_async_copy(counts_hbm.at[:, shard, :], counts, load_sem.at[2])
    load_hist = pltpu.make_async_copy(hist_hbm, cache.at[:, :, x, mine, :], load_sem.at[3])
    load_lengths = pltpu.make_async_copy(lengths_hbm, lengths, load_sem.at[4])
    for load in (load_ids, load_counts, load_lengths, *map(table_load, range(table_loads)), load_hist):
        load.start()
    sources = (w_in_hbm, w_out_hbm, w_proj_hbm, w_back_hbm)
    targets = (w_in, w_out, w_proj, w_back)
    weight_loads = [pltpu.make_async_copy(s, d, weight_sem.at[i]) for i, (s, d) in enumerate(zip(sources, targets))]

    barrier = pltpu.get_barrier_semaphore()
    for dz, dc in steps[:-1]:
        pl.semaphore_signal(barrier, inc=1, device_id={"table": table_peer(dz, dc)}, device_id_type=MESH)
    for d in x_far:
        pl.semaphore_signal(barrier, inc=1, device_id={"seq_0": (x + d) % seq_0}, device_id_type=MESH)
    for d in y_far:
        pl.semaphore_signal(barrier, inc=1, device_id={"seq_1": (y + d) % seq_1}, device_id_type=MESH)

    load_ids.wait()
    ids_low[...] = ids_in[...] & (vocab - 1)
    move_ids = pltpu.make_async_copy(ids_low, ids, load_sem.at[0])
    move_ids.start()
    load_counts.wait()
    load_lengths.wait()

    def offset_row(t, carry):
        total = jnp.int32(0)
        for g in range(groups):
            offsets[t, g] = total
            total = total + counts[t, g]
        return carry

    lax.fori_loop(0, groups, offset_row, 0)
    block = 256
    eye = identity(block, block, jnp.bfloat16)
    blank = jnp.zeros((128 - columns, block), jnp.bfloat16)

    def widen(b, carry):
        table_load(b).wait()
        for k in range(WIDEN):
            at = pl.multiple_of((b * WIDEN + k) * 2 * block, 2 * block)
            piece = jnp.concatenate(
                [lanes_in[:, pl.ds(at, block)], blank, lanes_in[:, pl.ds(at + block, block)], blank], axis=0
            )
            turned = dot_nt(eye, piece)
            wide[pl.ds(at, block), :] = turned[:, :128]
            wide[pl.ds(at + block, block), :] = turned[:, 128:]
        return carry

    lax.fori_loop(0, table_loads, widen, 0)
    for load in weight_loads:
        load.start()

    load_hist.wait()
    pl.semaphore_wait(barrier, len(steps) - 1 + len(x_far) + len(y_far))

    def hist_copy(n, view, axis, to):
        return pltpu.make_async_remote_copy(
            src_ref=view,
            dst_ref=view,
            send_sem=hist_send.at[n],
            recv_sem=hist_recv.at[n],
            device_id={axis: to},
            device_id_type=MESH,
        )

    own_keys = cache.at[:, 0, x, mine, :]
    own_vals = cache.at[:, 1, x, mine, :]
    row_keys = cache.at[:, 0, x, :, :]
    row_vals = cache.at[:, 1, :, mine, :]
    first, second = [], []
    for d in y_far:
        first.append(hist_copy(len(first), own_keys, "seq_1", (y + d) % seq_1))
    for d in x_far:
        first.append(hist_copy(len(first), own_vals, "seq_0", (x + d) % seq_0))
    for d in x_far:
        second.append(hist_copy(len(first) + len(second), row_keys, "seq_0", (x + d) % seq_0))
    for d in y_far:
        second.append(hist_copy(len(first) + len(second), row_vals, "seq_1", (y + d) % seq_1))
    for copy in first:
        copy.start()

    fold = identity(columns, 128, jnp.bfloat16)
    slot_iota = lax.broadcasted_iota(jnp.int32, (cap, 128), 0)

    def own_copy(j):
        here = emb.at[pl.ds(table_index * columns, columns), pl.ds(j * chunk_slots, chunk_slots)]
        return pltpu.make_async_copy(outgoing.at[j, len(steps) - 1], here, own_sem.at[j])

    def piece_copy(j, n):
        dz, dc = steps[n]
        return pltpu.make_async_remote_copy(
            src_ref=outgoing.at[j, n],
            dst_ref=emb.at[pl.ds(table_index * columns, columns), pl.ds(j * chunk_slots, chunk_slots)],
            send_sem=piece_send.at[j, n],
            recv_sem=piece_recv.at[j, n],
            device_id={"table": table_peer(dz, dc)},
            device_id_type=MESH,
        )

    move_ids.wait()
    id_rows = chunk_rows // 128
    places = [table_index // groups + u for u in range(TAKE)]

    def send(j):
        for n in range(len(steps) - 1):
            piece_copy(j, n).start()
        own_copy(j).start()

    def chunk(j, carry):
        def take(i, inner):
            for v in range(128 // TAKE):
                some = ids.at[j * id_rows + i, pl.ds(v * TAKE, TAKE)]
                into = rows.at[pl.ds(pl.multiple_of(i * 128 + v * TAKE, TAKE), TAKE), :]
                for u in range(TAKE):
                    into[u : u + 1, :] = wide[pl.ds(some[places[u]], 1), :]
            return inner

        lax.fori_loop(0, id_rows, take, 0)

        @pl.when(j == 1)
        def _():
            for copy in first:
                copy.wait()
            for copy in second:
                copy.start()

        for n, (dz, dc) in enumerate(steps):
            g = table_peer(dz, dc)
            for t in range(senders):
                sender = j * senders + t
                start = offsets[sender, g]
                filled = counts[sender, g]
                taken = rows[pl.ds(start + t * per_sender, cap), :]
                window[n % 2, t * cap : (t + 1) * cap, :] = jnp.where(slot_iota < filled, taken, 0.0).astype(jnp.bfloat16)
            outgoing[j, n] = dot_nt(fold, window[n % 2]).astype(jnp.bfloat16)

        @pl.when(j == 0)
        def _():
            send(j)

        @pl.when(j > 1)
        def _():
            send(j - 1)

        return carry

    lax.fori_loop(0, CHUNKS, chunk, 0)

    for load in weight_loads:
        load.wait()
    turn = identity(chunk_slots, chunk_slots, jnp.bfloat16)

    def block_rows(j):
        return pl.ds(pl.multiple_of(j * chunk_slots, chunk_slots), chunk_slots)

    def arrive(j):
        for n in range(len(steps) - 1):
            piece_copy(j, n).wait()
        own_copy(j).wait()

    def content(j):
        content_in = dot_nt(turn, emb[:, block_rows(j)]).astype(jnp.bfloat16)
        out[block_rows(j), :] = content_block(content_in, w_in, w_out, hidden)

    arrive(0)
    send(CHUNKS - 1)
    content(0)
    for copy in second:
        copy.wait()
    build_caches(cache, keys, vals, lengths[table_index])

    def run(j, carry):
        @pl.when(j > 0)
        def _():
            arrive(j)
            content(j)

        out[block_rows(j), :] = layers_block(out[block_rows(j), :], w_proj, w_back, keys, vals, weights)
        return carry

    lax.fori_loop(0, CHUNKS, run, 0)


def local(item_ids, item_table, group_counts, lengths, history, w_in, w_out, w_proj, w_back):
    groups = lax.axis_size("table")
    seq_0, seq_1 = lax.axis_size("seq_0"), lax.axis_size("seq_1")
    vocab, columns = item_table.shape
    per_sender = item_ids.shape[0] // groups
    cap = 3 * per_sender // (2 * groups)
    layers, hist_rows, width = history.shape[1], history.shape[3], history.shape[4]
    hist = hist_rows * seq_0 * seq_1
    slots = groups * cap
    senders = groups // CHUNKS
    block = senders * cap
    dims = (groups, seq_0, seq_1, vocab, columns, per_sender, cap, hist_rows)
    id_rows = item_ids.shape[0] // 128
    in_hbm = pl.BlockSpec(memory_space=pltpu.HBM)
    vmem, dma = pltpu.VMEM, pltpu.SemaphoreType.DMA
    operands = (lengths, item_ids.reshape(id_rows, 128), group_counts, item_table.T, history[0], w_in, w_out, w_proj, w_back)
    operands = [pltpu.with_memory_space_constraint(a, pltpu.HBM) for a in operands]
    return pl.pallas_call(
        functools.partial(rank_kernel, dims),
        out_shape=jax.ShapeDtypeStruct((slots, width), jnp.bfloat16),
        in_specs=[in_hbm] * 9,
        out_specs=pl.BlockSpec(memory_space=pltpu.VMEM),
        scratch_shapes=[
            vmem((vocab, 128), jnp.float32),
            vmem((columns, vocab), jnp.bfloat16),
            vmem((id_rows, 128), jnp.int32),
            vmem((id_rows, 128), jnp.int32),
            pltpu.SMEM((id_rows, 128), jnp.int32),
            pltpu.SMEM((groups, groups), jnp.int32),
            pltpu.SMEM((groups,), jnp.int32),
            pltpu.SMEM((groups, groups), jnp.int32),
            vmem((senders * per_sender + 128, 128), jnp.float32),
            vmem((2, block, 128), jnp.bfloat16),
            vmem((CHUNKS, groups, columns, block), jnp.bfloat16),
            vmem((width, slots), jnp.bfloat16),
            vmem((layers, 2, seq_0, seq_1 * hist_rows, width), jnp.bfloat16),
            vmem(w_in.shape, jnp.bfloat16),
            vmem(w_out.shape, jnp.bfloat16),
            vmem(w_proj.shape, jnp.bfloat16),
            vmem(w_back.shape, jnp.bfloat16),
            vmem((layers, HEADS, hist, 2 * HEAD_DIM), jnp.bfloat16),
            vmem((layers, HEADS // 2, 2 * hist, 2 * HEAD_DIM), jnp.bfloat16),
            vmem((block, w_in.shape[1]), jnp.bfloat16),
            vmem((2, 2, block, hist), jnp.bfloat16),
            dma((5,)),
            dma((vocab // (512 * WIDEN),)),
            dma((4,)),
            dma((CHUNKS, groups)),
            dma((CHUNKS, groups)),
            dma((2 * (seq_0 + seq_1 - 2),)),
            dma((2 * (seq_0 + seq_1 - 2),)),
            dma((CHUNKS,)),
        ],
        compiler_params=pltpu.CompilerParams(
            collective_id=0, has_side_effects=True, vmem_limit_bytes=50 * 1024 * 1024
        ),
        name="rank",
    )(*operands)


def solution(mesh):
    torus = Mesh(mesh.devices.reshape(mesh.shape["table"], 4, 4), ("table", "seq_0", "seq_1"))
    in_specs = (
        P(SEQ),
        P(SEQ, "table"),
        P(),
        P(),
        P("table", None, None, SEQ, None),
        P(),
        P(),
        P(),
        P(),
    )
    out_specs = P(TABLE_SEQ, None)
    return jax.shard_map(local, mesh=torus, in_specs=in_specs, out_specs=out_specs, check_vma=False)
```
